256 devices in a mesh: grp: 16 (over z, x_hi), wide: 16 (over y, x_lo, core).
Axes of the slice: x: 4 (x_hi: 2, x_lo: 2; x = x_hi * 2 + x_lo), y: 4, z: 8, core: 2. Of those that a mesh axis runs over, the one named last changes fastest.
Arguments:
- velocity: float32 [3, 1024, 128, 128], P(None, 'grp', 'wide'), may hold values from -6 to 6
- coarse_ghost: float32 [3, 1024, 32, 128], P(None, 'grp', 'wide'), may hold values from -6 to 6
- viscosity: float32 [1024, 128, 128], P('grp', 'wide'), may hold values from 0.5 to 4
- stress: float32 [6, 1024, 128, 128], P(None, 'grp', 'wide'), may hold values from -6 to 6
- patch_mask: int32 [16, 32], P('grp', 'wide'), may hold values 0 or 1
- coarse_owner: int32 [16, 32], P('grp', 'wide'), may hold values from 0 to 255, as said below
Outputs:
- new_velocity: float32 [3, 1024, 128, 128], P(None, 'grp', 'wide')
- coarse_patch_update: float32 [16, 256, 3, 6144], P('grp', 'wide')
The draws below stay inside these ranges and needn't reach their ends.
Inputs may be any that keep to these rules, and one draw needn't show every extreme that they name: `coarse_owner`: coarse patch c belongs to wide index c // 16. Of the 2 fine patches of one device at most 1 have coarse patches on any one wide index, and in every draw every device sends exactly 1 to one common wide index.
All inputs are finite; a program needn't handle non-finite values. No bound on the sum of `patch_mask` on one device may be relied on, other than what follows from the above.
Results may differ from the reference program's by a relative error of at most 0.000096.
Values sent between devices are 32-bit elements; how exact they have to be, the bound alone decides.
A program may use at most 128 MiB of HBM per device.

```python
import math
import jax
import jax.numpy as jnp
from jax import lax

PATCH = 64
CY = 8
P_SIZE = 2
CP_DEV = 16
SWEEPS = 3
CAP = 1
CZ = 128
NX = 1024
NY = 128
PV = 6144
CPW = 256
N_GRP = 16
N_WIDE = 16


def draw_coarse_owner(key, part):
    slot_count = N_WIDE * CAP
    favoured = jax.random.randint(jax.random.fold_in(key, 11), (), 0, N_WIDE)

    def one_device(device_index):
        dev_key = jax.random.fold_in(key, 100 + device_index)
        ranks = jax.random.permutation(jax.random.fold_in(dev_key, 1), slot_count)
        slot_ids = jnp.arange(slot_count)
        scores = jnp.where(slot_ids // CAP == favoured, slot_ids - slot_count, ranks)
        chosen = jnp.argsort(scores, stable=True)[:P_SIZE]
        chosen = jax.random.permutation(jax.random.fold_in(dev_key, 2), chosen)
        local_ids = jax.random.randint(jax.random.fold_in(dev_key, 3), (P_SIZE,), 0, CP_DEV)
        return chosen // CAP * CP_DEV + local_ids
    table = jax.vmap(one_device)(jnp.arange(N_GRP * N_WIDE))
    return table.reshape(N_GRP, N_WIDE * P_SIZE).astype(jnp.int32)


def plant(values, own_key, smallest, top_value):
    index_at = [jax.random.randint(jax.random.fold_in(own_key, axis), (), 0, length) for axis, length in enumerate(values.shape)]
    main_axis = values.shape.index(max(values.shape))
    next_to = index_at[:main_axis] + [(index_at[main_axis] + 1) % values.shape[main_axis]] + index_at[main_axis + 1:]
    return values.at[tuple(index_at)].set(smallest).at[tuple(next_to)].set(top_value)


def block_scale(key, extent, shards, least, top_value):
    level, own = 1.0, jax.random.fold_in(key, 6)
    for axis_at, parts in shards:
        steps = jnp.exp(jax.random.uniform(jax.random.fold_in(own, axis_at), (parts,), jnp.float32, least / len(shards), top_value / len(shards)))
        level = level * jnp.repeat(steps, extent[axis_at] // parts).reshape([-1 if axis == axis_at else 1 for axis in range(len(extent))])
    return level


def scatter_about(stream_key, extent, scale, most, pieces=(), kind=jnp.bfloat16):
    entries = scale * jax.random.normal(stream_key, extent, jnp.float32)
    if pieces:
        entries = entries * block_scale(stream_key, extent, pieces, -0.22, 0.18)
    return jnp.clip(entries, -most, most).astype(kind)


def setup_inputs(seed: int = 0) -> dict:
    key_of = jax.random.split(jax.random.key(seed), 7)
    return {
        "velocity": scatter_about(key_of[0], (3, NX, NY, CZ), 1.0, 6.0, ((1, 16), (2, 16)), jnp.float32),
        "coarse_ghost": scatter_about(key_of[1], (3, NX, 2 * N_WIDE, CZ), 1.0, 6.0, ((1, 16), (2, 16)), jnp.float32),
        "viscosity": jnp.clip(jnp.exp(math.log(4.0) - 2.0794415 * jax.random.uniform(key_of[2], (NX, NY, CZ), jnp.float32) ** block_scale(key_of[2], (NX, NY, CZ), ((0, 16), (1, 16)), -0.2, 0.2)), 0.5, 4.0),
        "stress": scatter_about(key_of[3], (6, NX, NY, CZ), 1.0, 6.0, ((1, 16), (2, 16)), jnp.float32),
        "patch_mask": plant((jax.random.randint(key_of[4], (N_GRP, N_WIDE * P_SIZE), 0, 4) < 3).astype(jnp.int32), jax.random.fold_in(key_of[4], 1), 0, 1),
        "coarse_owner": draw_coarse_owner(jax.random.fold_in(key_of[6], 71), 0),
    }


KAPPA = 1.0
OMEGA = 0.8


def apply_operator(values_in, visc_pad):
    centre_cell = visc_pad[1:-1, 1:-1]
    visc_east = 0.5 * (centre_cell + visc_pad[2:, 1:-1])
    visc_west = 0.5 * (centre_cell + visc_pad[:-2, 1:-1])
    visc_north = 0.5 * (centre_cell + visc_pad[1:-1, 2:])
    visc_south = 0.5 * (centre_cell + visc_pad[1:-1, :-2])
    visc_up = 0.5 * (centre_cell + jnp.roll(centre_cell, -1, axis=2))
    visc_down = 0.5 * (centre_cell + jnp.roll(centre_cell, 1, axis=2))
    interior = values_in[:, 1:-1, 1:-1]
    diffusion = visc_east * (values_in[:, 2:, 1:-1] - interior) - visc_west * (interior - values_in[:, :-2, 1:-1])
    diffusion = diffusion + visc_north * (values_in[:, 1:-1, 2:] - interior) - visc_south * (interior - values_in[:, 1:-1, :-2])
    diffusion = diffusion + visc_up * (jnp.roll(interior, -1, axis=3) - interior) - visc_down * (interior - jnp.roll(interior, 1, axis=3))
    diagonal = KAPPA + visc_east + visc_west + visc_north + visc_south + visc_up + visc_down
    return KAPPA * interior - diffusion, diagonal


def divergence(stress_pad):
    def diff_x(comp):
        return 0.5 * (comp[2:, 1:-1] - comp[:-2, 1:-1])

    def diff_y(comp):
        return 0.5 * (comp[1:-1, 2:] - comp[1:-1, :-2])

    def diff_z(comp):
        middle = comp[1:-1, 1:-1]
        return 0.5 * (jnp.roll(middle, -1, axis=2) - jnp.roll(middle, 1, axis=2))

    force_x = diff_x(stress_pad[0]) + diff_y(stress_pad[3]) + diff_z(stress_pad[4])
    force_y = diff_x(stress_pad[3]) + diff_y(stress_pad[1]) + diff_z(stress_pad[5])
    force_z = diff_x(stress_pad[4]) + diff_y(stress_pad[5]) + diff_z(stress_pad[2])
    return jnp.stack([force_x, force_y, force_z], axis=0)


def patch_data(residual, smoothed, viscosity, coarse_ghost, groups):
    half = PATCH // 2
    blocks = residual.reshape(3, groups, half, 2, CY // 2, 2, P_SIZE, half, 2).mean(axis=(3, 5, 8))
    blocks = jnp.transpose(blocks, (1, 4, 0, 2, 3, 5)).reshape(groups, P_SIZE, 3, half * (CY // 2) * half)
    flux_low = viscosity[:, 0, :] * (smoothed[:, :, 0, :] - coarse_ghost[:, :, 0, :])
    flux_high = viscosity[:, -1, :] * (coarse_ghost[:, :, 1, :] - smoothed[:, :, -1, :])

    def faces(flux):
        reduced_terms = flux.reshape(3, groups, half, 2, P_SIZE, half, 2).mean(axis=(3, 6))
        return jnp.transpose(reduced_terms, (1, 3, 0, 2, 4)).reshape(groups, P_SIZE, 3, half * half)

    return jnp.concatenate([blocks, faces(flux_low), faces(flux_high)], axis=3)


def column(velocity, coarse_ghost, viscosity, stress):
    vel_field = jnp.concatenate([coarse_ghost[:, :, :1], velocity, coarse_ghost[:, :, 1:]], axis=2)
    vel_field = jnp.pad(vel_field, ((0, 0), (1, 1), (0, 0), (0, 0)))
    visc_pad = jnp.concatenate([viscosity[:, :1], viscosity, viscosity[:, -1:]], axis=1)
    visc_pad = jnp.pad(visc_pad, ((1, 1), (0, 0), (0, 0)))
    stress_pad = jnp.pad(stress, ((0, 0), (1, 1), (1, 1), (0, 0)))
    source = KAPPA * velocity + divergence(stress_pad)
    for sweep_index in range(SWEEPS):
        applied, diagonal = apply_operator(vel_field, visc_pad)
        interior = vel_field[:, 1:-1, 1:-1]
        updated = interior + OMEGA * (source - applied) / diagonal
        vel_field = vel_field.at[:, 1:-1, 1:-1].set(updated)
    applied, diagonal = apply_operator(vel_field, visc_pad)
    residual = source - applied
    smoothed = vel_field[:, 1:-1, 1:-1]
    return smoothed, patch_data(residual, smoothed, viscosity, coarse_ghost, N_GRP)


def reference(velocity, coarse_ghost, viscosity, stress, patch_mask, coarse_owner):
    vel_cols = jnp.moveaxis(velocity.reshape(3, NX, N_WIDE, CY, CZ), 2, 0)
    ghost_cols = jnp.moveaxis(coarse_ghost.reshape(3, NX, N_WIDE, 2, CZ), 2, 0)
    visc_cols = jnp.moveaxis(viscosity.reshape(NX, N_WIDE, CY, CZ), 1, 0)
    stress_cols = jnp.moveaxis(stress.reshape(6, NX, N_WIDE, CY, CZ), 2, 0)
    smoothed, fine_patches = lax.map(lambda items: column(*items), (vel_cols, ghost_cols, visc_cols, stress_cols))
    new_velocity = jnp.moveaxis(smoothed, 0, 2).reshape(3, NX, NY, CZ)
    fine_patches = jnp.transpose(fine_patches, (1, 0, 2, 3, 4)).reshape(N_GRP, N_WIDE * P_SIZE, 3 * PV)
    fine_patches = fine_patches * patch_mask[:, :, None].astype(jnp.float32)
    indicator_matrix = (coarse_owner[:, None, :] == jnp.arange(CPW, dtype=jnp.int32)[None, :, None]).astype(jnp.float32)
    coarse_patch_update = jnp.einsum("xjn,xnd->xjd", indicator_matrix, fine_patches, precision=lax.Precision.HIGHEST)
    return new_velocity, coarse_patch_update.reshape(N_GRP, CPW, 3, PV)
```

```python
import functools

import jax
import jax.numpy as jnp
from jax import lax
from jax.experimental import pallas as pl
from jax.experimental.pallas import tpu as pltpu
from jax.sharding import PartitionSpec as P

MESH = pl.DeviceIdType.MESH
F32 = jnp.float32

NX = 64
M = 4
EX = NX + 2 * M
KAPPA = 1.0
OMEGA = 0.8
CP_DEV = 16

CHUNKS = (
    (0, 40, ((0, 2, 8), (8, 10, 8), (16, 18, 8), (24, 26, 4), (28, 33, 6), (34, 41, 6))),
    (120, 8, ((0, 0, 2), (2, 30, 2), (4, 32, 1), (5, 39, 1), (6, 40, 1), (7, 47, 1))),
)


def step_kernel(
    n_grp, n_wide,
    mask_ref, owner_ref, vel_hbm, ghost_hbm, visc_hbm, stress_hbm,
    newvel_hbm, recv_hbm, labels_hbm,
    u0, st, vi, gh, fe, fw, fn, fs, fu, fd, ww, dd, ve, sp, gv, u1, u2, u3, rs, fl,
    lhs, mat, slots, lab,
    in_sem, halo_send, halo_recv, lab_send, lab_recv, pay_send, pay_recv, out_sem,
):
    g = lax.axis_index("grp")
    wd = lax.axis_index("wide")
    up = lax.rem(g + 1, n_grp)
    down = lax.rem(g + n_grp - 1, n_grp)

    loads = [
        pltpu.make_async_copy(vel_hbm, u0.at[:, pl.ds(M, NX)], in_sem.at[0]),
        pltpu.make_async_copy(stress_hbm, st.at[:, pl.ds(M, NX)], in_sem.at[1]),
        pltpu.make_async_copy(visc_hbm, vi.at[pl.ds(M, NX)], in_sem.at[2]),
        pltpu.make_async_copy(ghost_hbm, gh.at[:, pl.ds(M, NX)], in_sem.at[3]),
    ]
    for copy in loads:
        copy.start()

    barrier = pltpu.get_barrier_semaphore()
    for other in (up, down):
        pl.semaphore_signal(barrier, inc=1, device_id=(other, wd), device_id_type=MESH)
    for d in range(1, n_wide):
        pl.semaphore_signal(
            barrier, inc=1, device_id=(g, lax.rem(wd + d, n_wide)), device_id_type=MESH
        )
    lane = lax.broadcasted_iota(jnp.int32, (1, 128), 1)
    lab[...] = jnp.where(lane == 0, owner_ref[0, 0], owner_ref[0, 1])
    pl.semaphore_wait(barrier, n_wide + 1)

    halos = []
    for side, (other, src, dst) in enumerate(((up, NX - M, 0), (down, 0, M + NX))):
        pairs = (
            (vel_hbm.at[:, pl.ds(src, M)], u0.at[:, pl.ds(dst, M)]),
            (visc_hbm.at[pl.ds(src, M)], vi.at[pl.ds(dst, M)]),
            (stress_hbm.at[:, pl.ds(src, M)], st.at[:, pl.ds(dst, M)]),
            (ghost_hbm.at[:, pl.ds(src, M)], gh.at[:, pl.ds(dst, M)]),
        )
        for i, (s, t) in enumerate(pairs):
            halos.append(
                pltpu.make_async_remote_copy(
                    src_ref=s, dst_ref=t,
                    send_sem=halo_send.at[side, i], recv_sem=halo_recv.at[side, i],
                    device_id=(other, wd), device_id_type=MESH,
                )
            )
    for copy in halos:
        copy.start()

    def label_copy(d):
        return pltpu.make_async_remote_copy(
            src_ref=lab, dst_ref=labels_hbm.at[d],
            send_sem=lab_send.at[d], recv_sem=lab_recv.at[d],
            device_id=(g, lax.rem(wd + d, n_wide)), device_id_type=MESH,
        )

    for d in range(1, n_wide):
        label_copy(d).start()
    own_label = pltpu.make_async_copy(lab, labels_hbm.at[0], out_sem.at[1])
    own_label.start()

    row = lax.broadcasted_iota(jnp.int32, (512, 256), 0)
    col = lax.broadcasted_iota(jnp.int32, (512, 256), 1)
    same_q = lax.shift_right_logical(row, 7) == (lax.shift_right_logical(col, 5) & 3)
    z_pair = lax.shift_right_logical(row & 127, 1)
    z_want = lax.shift_right_logical(col, 7) * 32 + (col & 31)
    mat[...] = jnp.where(same_q & (z_pair == z_want), 1.0, 0.0).astype(jnp.bfloat16)

    ypos = lax.broadcasted_iota(jnp.int32, (1, 8, 128), 1)
    not_last = ypos < 7
    not_first = ypos > 0

    def y_up(a):
        return pltpu.roll(a, 7, 1)

    def y_dn(a):
        return pltpu.roll(a, 1, 1)

    def z_up(a):
        return pltpu.roll(a, 127, 2)

    def z_dn(a):
        return pltpu.roll(a, 1, 2)

    def prep(lo, n, inside=None):
        here, after, before = pl.ds(lo, n), pl.ds(lo + 1, n), pl.ds(lo - 1, n)
        v = vi[here]
        f_e = 0.5 * (v + vi[after])
        f_w = 0.5 * (v + vi[before])
        f_n = jnp.where(not_last, 0.5 * (v + y_up(v)), 0.0)
        f_s = y_dn(f_n)
        f_u = 0.5 * (v + z_up(v))
        f_d = z_dn(f_u)
        v_edge = jnp.where(not_last & not_first, 0.0, v)
        diag = KAPPA + f_e + f_w + f_n + f_s + f_u + f_d + v_edge
        weight = OMEGA / diag
        if inside is not None:
            weight = weight * inside
        fe[here], fw[here], fn[here], fs[here], fu[here], fd[here] = f_e, f_w, f_n, f_s, f_u, f_d
        ww[here], dd[here] = weight, diag
        ve[here] = v_edge

        def d_x(c):
            return st[c, after] - st[c, before]

        def d_y(a):
            return jnp.where(not_last, y_up(a), 0.0) - jnp.where(not_first, y_dn(a), 0.0)

        def d_z(a):
            return z_up(a) - z_dn(a)

        ghost_edges = []
        for c in range(3):
            low = jnp.broadcast_to(gh[c, here, 0:1, :], (n, 8, 128))
            high = jnp.broadcast_to(gh[c, here, 1:2, :], (n, 8, 128))
            edge = jnp.where(not_first, jnp.where(not_last, 0.0, high), low)
            gv[c, here] = edge
            ghost_edges.append(v_edge * edge)
        sxy, sxz, syz = st[3, here], st[4, here], st[5, here]
        sp[0, here] = u0[0, here] + 0.5 * (d_x(0) + d_y(sxy) + d_z(sxz)) + ghost_edges[0]
        sp[1, here] = u0[1, here] + 0.5 * (d_x(3) + d_y(st[1, here]) + d_z(syz)) + ghost_edges[1]
        sp[2, here] = u0[2, here] + 0.5 * (d_x(4) + d_y(syz) + d_z(st[2, here])) + ghost_edges[2]

    def flow(src, lo, n):
        here, after, before = pl.ds(lo, n), pl.ds(lo + 1, n), pl.ds(lo - 1, n)
        f_e, f_w, f_n, f_s, f_u, f_d = fe[here], fw[here], fn[here], fs[here], fu[here], fd[here]
        for c in range(3):
            u = src[c, here]
            total = (
                (sp[c, here] + f_e * src[c, after] + f_w * src[c, before])
                + (f_n * y_up(u) + f_s * y_dn(u))
                + (f_u * z_up(u) + f_d * z_dn(u))
            )
            yield c, u, total

    def sweep(src, dst, lo, n):
        here = pl.ds(lo, n)
        weight = ww[here]
        for c, u, total in flow(src, lo, n):
            dst[c, here] = (1.0 - OMEGA) * u + weight * total

    def restrict(lo, n):
        here = pl.ds(lo, n)
        diag, v_edge = dd[here], ve[here]
        half = n // 2
        pairs = pl.ds(pl.multiple_of((lo - M) * 4, 8), half * 8)
        for c, u, total in flow(u3, lo, n):
            res = (total - diag * u).reshape(half, 2, 8, 128)
            res = res[:, 0] + res[:, 1]
            res = res + y_up(res)
            rs[c, pairs] = res.reshape(half * 8, 128)
            flux = (v_edge * (u - gv[c, here])).reshape(half, 2, 8, 128)
            fl[c, pairs] = (flux[:, 0] + flux[:, 1]).reshape(half * 8, 128)

    def over(fn_, lo, hi, n):
        count = (hi - lo) // n

        def body(i, carry):
            fn_(lo + i * n, n)
            return carry

        lax.fori_loop(0, count, body, 0)
        if (hi - lo) % n:
            fn_(lo + count * n, (hi - lo) % n)

    mask0 = mask_ref[0, 0].astype(F32)
    mask1 = mask_ref[0, 1].astype(F32)
    target0 = owner_ref[0, 0] // CP_DEV
    target1 = owner_ref[0, 1] // CP_DEV

    def payload_copy(chunk, d):
        base, rows, _ = CHUNKS[chunk]
        return pltpu.make_async_remote_copy(
            src_ref=slots.at[d, pl.ds(base, 3 * rows)],
            dst_ref=recv_hbm.at[d, pl.ds(base, 3 * rows)],
            send_sem=pay_send.at[chunk, d], recv_sem=pay_recv.at[chunk, d],
            device_id=(g, lax.rem(wd + d, n_wide)), device_id_type=MESH,
        )

    def own_copy(chunk):
        base, rows, _ = CHUNKS[chunk]
        return pltpu.make_async_copy(
            slots.at[0, pl.ds(base, 3 * rows)], recv_hbm.at[0, pl.ds(base, 3 * rows)],
            out_sem.at[2 + chunk],
        )

    def send(chunk):
        base, rows, segments = CHUNKS[chunk]
        for c in range(3):
            for at, tile, count in segments:
                for q in range(4):
                    if tile < 32:
                        piece = rs[c, pl.ds(tile * 8 + 2 * q, count, stride=8), :] * 0.125
                    else:
                        fr, y, sign = (tile - 32, 0, 0.25) if tile < 40 else (tile - 40, 7, -0.25)
                        piece = fl[c, pl.ds(fr * 32 + q * 8 + y, count, stride=32), :] * sign
                    lhs[pl.ds(c * rows + at, count), pl.ds(q * 128, 128)] = piece
        full = lhs[pl.ds(0, 3 * rows), :]
        high = full.astype(jnp.bfloat16)
        low = (full - high.astype(F32)).astype(jnp.bfloat16)
        m = mat[...]
        out = jnp.dot(high, m, preferred_element_type=F32) + jnp.dot(
            low, m, preferred_element_type=F32
        )
        p0 = out[:, :128] * mask0
        p1 = out[:, 128:] * mask1
        for d in range(n_wide):
            t = lax.rem(wd + d, n_wide)
            s0 = jnp.where(target0 == t, 1.0, 0.0)
            s1 = jnp.where(target1 == t, 1.0, 0.0)
            slots[d, pl.ds(base, 3 * rows), :] = p0 * s0 + p1 * s1
            if d:
                payload_copy(chunk, d).start()
            else:
                own_copy(chunk).start()

    for copy in loads:
        copy.wait()

    over(prep, M + 1, M + NX - 1, 4)
    over(functools.partial(sweep, u0, u1), M + 1, M + NX - 1, 4)
    over(functools.partial(sweep, u1, u2), M + 2, M + NX - 2, 4)
    over(functools.partial(sweep, u2, u3), M + 3, M + NX - 3, 4)
    over(restrict, M + 4, M + NX - 4, 4)
    send(0)

    for copy in halos:
        copy.wait()
    inside_low = jnp.where(g > 0, 1.0, 0.0)
    inside_high = jnp.where(g < n_grp - 1, 1.0, 0.0)
    for at, inside in ((0, inside_low), (M + NX, inside_high)):
        here = pl.ds(at, M)
        u0[:, here] = u0[:, here] * inside
        st[:, here] = st[:, here] * inside
        vi[here] = vi[here] * inside
    prep(1, 3, inside_low)
    prep(M, 1)
    prep(M + NX - 1, 1)
    prep(M + NX, 3, inside_high)
    for src, dst, shift in ((u0, u1, 1), (u1, u2, 2), (u2, u3, 3)):
        sweep(src, dst, shift, 4)
        sweep(src, dst, EX - 4 - shift, 4)
    store = pltpu.make_async_copy(u3.at[:, pl.ds(M, NX)], newvel_hbm, out_sem.at[0])
    store.start()
    restrict(M, 4)
    restrict(M + NX - 4, 4)
    send(1)

    for d in range(1, n_wide):
        label_copy(d).wait()
        for chunk in range(2):
            payload_copy(chunk, d).wait()
    own_label.wait()
    own_copy(0).wait()
    own_copy(1).wait()
    store.wait()


def sum_kernel(n_wide, labels_ref, vel_hbm, recv_hbm, newvel_hbm, out_ref, recv, sems):
    me = lax.axis_index("wide")
    move = pltpu.make_async_copy(vel_hbm, newvel_hbm, sems.at[0])
    fetch = pltpu.make_async_copy(recv_hbm, recv, sems.at[1])
    fetch.start()
    move.start()
    out_ref[...] = jnp.zeros_like(out_ref)
    fetch.wait()
    for d in range(n_wide):
        first, second = labels_ref[d, 0, 0], labels_ref[d, 0, 1]
        hit0 = first // CP_DEV == me
        hit1 = second // CP_DEV == me
        index = jnp.where(hit0, first, second) % CP_DEV

        @pl.when(hit0 | hit1)
        def _():
            start = (index // 8) * 384 + index % 8
            for base, rows, segments in CHUNKS:
                for c in range(3):
                    for at, tile, count in segments:
                        where = pl.ds(start + c * 768 + tile * 8, count, stride=8)
                        out_ref[where, :] = (
                            out_ref[where, :] + recv[d, pl.ds(base + c * rows + at, count), :]
                        )

    move.wait()


def on_device(velocity, coarse_ghost, viscosity, stress, patch_mask, coarse_owner):
    n_grp, n_wide = lax.axis_size("grp"), lax.axis_size("wide")
    hbm = pl.BlockSpec(memory_space=pltpu.HBM)
    smem = pl.BlockSpec(memory_space=pltpu.SMEM)
    scalar_field = pltpu.VMEM((EX, 8, 128), F32)
    field = pltpu.VMEM((3, EX, 8, 128), F32)
    new_velocity, received, labels = pl.pallas_call(
        functools.partial(step_kernel, n_grp, n_wide),
        out_shape=(
            jax.ShapeDtypeStruct((3, NX, 8, 128), F32),
            jax.ShapeDtypeStruct((n_wide, 144, 128), F32),
            jax.ShapeDtypeStruct((n_wide, 1, 128), jnp.int32),
        ),
        in_specs=[smem, smem, hbm, hbm, hbm, hbm],
        out_specs=(hbm, hbm, hbm),
        scratch_shapes=[
            field, pltpu.VMEM((6, EX, 8, 128), F32), scalar_field, pltpu.VMEM((3, EX, 2, 128), F32),
            *[scalar_field] * 9,
            field, field, field, field, field,
            pltpu.VMEM((3, 256, 128), F32), pltpu.VMEM((3, 256, 128), F32),
            pltpu.VMEM((120, 512), F32), pltpu.VMEM((512, 256), jnp.bfloat16),
            pltpu.VMEM((n_wide, 144, 128), F32), pltpu.VMEM((1, 128), jnp.int32),
            pltpu.SemaphoreType.DMA((4,)),
            pltpu.SemaphoreType.DMA((2, 4)), pltpu.SemaphoreType.DMA((2, 4)),
            pltpu.SemaphoreType.DMA((n_wide,)), pltpu.SemaphoreType.DMA((n_wide,)),
            pltpu.SemaphoreType.DMA((2, n_wide)), pltpu.SemaphoreType.DMA((2, n_wide)),
            pltpu.SemaphoreType.DMA((4,)),
        ],
        compiler_params=pltpu.CompilerParams(
            collective_id=0, has_side_effects=True, vmem_limit_bytes=40 << 20
        ),
        name="smooth_and_send",
    )(patch_mask, coarse_owner, velocity, coarse_ghost, viscosity, stress)
    new_velocity, coarse = pl.pallas_call(
        functools.partial(sum_kernel, n_wide),
        out_shape=(
            jax.ShapeDtypeStruct((3, NX, 8, 128), F32),
            jax.ShapeDtypeStruct((2304, 128), F32),
        ),
        in_specs=[smem, hbm, hbm],
        out_specs=(hbm, pl.BlockSpec(memory_space=pltpu.VMEM)),
        scratch_shapes=[pltpu.VMEM((n_wide, 144, 128), F32), pltpu.SemaphoreType.DMA((2,))],
        compiler_params=pltpu.CompilerParams(vmem_limit_bytes=40 << 20),
        name="sum_on_owners",
    )(labels, new_velocity, received)
    coarse = coarse.reshape(3, 2, 48, 8, 128).transpose(1, 3, 0, 2, 4)
    return new_velocity, coarse.reshape(1, CP_DEV, 3, 48 * 128)


def solution(mesh):
    in_specs = (
        P(None, "grp", "wide", None),
        P(None, "grp", "wide", None),
        P("grp", "wide", None),
        P(None, "grp", "wide", None),
        P("grp", "wide"),
        P("grp", "wide"),
    )
    out_specs = (P(None, "grp", "wide", None), P("grp", "wide", None, None))
    return jax.shard_map(
        on_device, mesh=mesh, in_specs=in_specs, out_specs=out_specs, check_vma=False
    )
```

```python
import functools

import jax
import jax.numpy as jnp
from jax import lax
from jax.experimental import pallas as pl
from jax.experimental.pallas import tpu as pltpu
from jax.sharding import PartitionSpec as P

MESH = pl.DeviceIdType.MESH
F32 = jnp.float32

NX = 64
M = 4
EX = NX + 2 * M
KAPPA = 1.0
OMEGA = 0.8
CP_DEV = 16
N_WIDE = 16
DX_COMPS = (0, 3, 4)

MAIN = (
    (0, 8, ((0, 2, 6), (6, 33, 1), (7, 41, 1))),
    (24, 16, ((0, 8, 8), (8, 16, 4), (12, 34, 2), (14, 42, 2))),
    (72, 16, ((0, 20, 8), (8, 28, 2), (10, 36, 3), (13, 44, 3))),
)
EDGE = (0, 8, ((0, 0, 2), (2, 30, 2), (4, 32, 1), (5, 39, 1), (6, 40, 1), (7, 47, 1)))


def step_kernel(
    n_grp,
    mask_hbm, owner_hbm, vel_hbm, ghost_hbm, visc_hbm, stress_hbm,
    newvel_hbm, main_hbm, edge_hbm, labels_hbm,
    u0, st, sx, vi, gh, fe, fw, fn, fs, fu, fd, ww, dd, ve, sp, gv, u1, u2, u3, rs, fl,
    lhs, mat, own, slots, lab, mask_ref, owner_ref,
    in_sem, halo_send, halo_recv, lab_send, lab_recv, edge_send, edge_recv, main_send, main_recv,
    out_sem,
):
    g = lax.axis_index("grp")
    wd = lax.axis_index("wide")
    up = lax.rem(g + 1, n_grp)
    down = lax.rem(g + n_grp - 1, n_grp)
    y, x, core = wd // 4, (wd // 2) % 2, wd % 2

    def wide_at(dy, fx, fc):
        return (
            ((y + dy) % 4) * 4
            + (1 - x if fx else x) * 2
            + (1 - core if fc else core)
        )

    others = [(dy, fx, fc) for dy in (2, 1, 3, 0) for fx in (1, 0) for fc in (0, 1)]
    others.remove((0, 0, 0))

    def slot_of(dy, fx, fc):
        return ((dy % 4) * 2 + fx) * 2 + fc

    loads = [
        pltpu.make_async_copy(visc_hbm, vi.at[pl.ds(M, NX)], in_sem.at[2]),
        pltpu.make_async_copy(stress_hbm, st.at[:, pl.ds(1, NX)], in_sem.at[1]),
        pltpu.make_async_copy(vel_hbm, u0.at[:, pl.ds(M, NX)], in_sem.at[0]),
        pltpu.make_async_copy(ghost_hbm, gh, in_sem.at[3]),
        pltpu.make_async_copy(owner_hbm, owner_ref, in_sem.at[4]),
        pltpu.make_async_copy(mask_hbm, mask_ref, in_sem.at[5]),
    ]
    for copy in loads:
        copy.start()

    barrier = pltpu.get_barrier_semaphore()
    for other in (up, down):
        pl.semaphore_signal(barrier, inc=1, device_id=(other, wd), device_id_type=MESH)
    for off in others:
        pl.semaphore_signal(barrier, inc=1, device_id=(g, wide_at(*off)), device_id_type=MESH)

    row = lax.broadcasted_iota(jnp.int32, (512, 256), 0)
    col = lax.broadcasted_iota(jnp.int32, (512, 256), 1)
    same_q = lax.shift_right_logical(row, 7) == (lax.shift_right_logical(col, 5) & 3)
    z_pair = lax.shift_right_logical(row & 127, 1)
    z_want = lax.shift_right_logical(col, 7) * 32 + (col & 31)
    mat[...] = jnp.where(same_q & (z_pair == z_want), 1.0, 0.0).astype(jnp.bfloat16)
    for comp in DX_COMPS:
        st[comp, 0] = jnp.zeros((8, 128), F32)
        st[comp, NX + 1] = jnp.zeros((8, 128), F32)

    ypos = lax.broadcasted_iota(jnp.int32, (1, 8, 128), 1)
    not_last = ypos < 7
    not_first = ypos > 0

    def y_up(a):
        return pltpu.roll(a, 7, 1)

    def y_dn(a):
        return pltpu.roll(a, 1, 1)

    def z_up(a):
        return pltpu.roll(a, 127, 2)

    def z_dn(a):
        return pltpu.roll(a, 1, 2)

    def faces(lo, n, inside=None):
        here, after, before = pl.ds(lo, n), pl.ds(lo + 1, n), pl.ds(lo - 1, n)
        v = vi[here]
        f_e = 0.5 * (v + vi[after])
        f_w = 0.5 * (v + vi[before])
        f_n = jnp.where(not_last, 0.5 * (v + y_up(v)), 0.0)
        f_s = y_dn(f_n)
        f_u = 0.5 * (v + z_up(v))
        f_d = z_dn(f_u)
        v_edge = jnp.where(not_last & not_first, 0.0, v)
        diag = KAPPA + f_e + f_w + f_n + f_s + f_u + f_d + v_edge
        weight = OMEGA / diag
        if inside is not None:
            weight = weight * inside
        fe[here], fw[here], fn[here], fs[here], fu[here], fd[here] = f_e, f_w, f_n, f_s, f_u, f_d
        ww[here], dd[here] = weight, diag

    def force(lo, n):
        here, own_rows = pl.ds(lo, n), pl.ds(lo - M, n)
        mid, after, before = pl.ds(lo - 3, n), pl.ds(lo - 2, n), pl.ds(lo - 4, n)
        v_edge = jnp.where(not_last & not_first, 0.0, vi[here])
        ve[here] = v_edge

        def d_x(c):
            return st[c, after] - st[c, before]

        def d_y(a):
            return jnp.where(not_last, y_up(a), 0.0) - jnp.where(not_first, y_dn(a), 0.0)

        def d_z(a):
            return z_up(a) - z_dn(a)

        sxy, sxz, syz = st[3, mid], st[4, mid], st[5, mid]
        slopes = (
            d_x(0) + d_y(sxy) + d_z(sxz),
            d_x(3) + d_y(st[1, mid]) + d_z(syz),
            d_x(4) + d_y(syz) + d_z(st[2, mid]),
        )
        for c in range(3):
            low = jnp.broadcast_to(gh[c, own_rows, 0:1, :], (n, 8, 128))
            high = jnp.broadcast_to(gh[c, own_rows, 1:2, :], (n, 8, 128))
            edge = jnp.where(not_first, jnp.where(not_last, 0.0, high), low)
            gv[c, here] = edge
            sp[c, here] = KAPPA * u0[c, here] + 0.5 * slopes[c] + v_edge * edge

    def flow(src, lo, n):
        here, after, before = pl.ds(lo, n), pl.ds(lo + 1, n), pl.ds(lo - 1, n)
        f_e, f_w, f_n, f_s, f_u, f_d = fe[here], fw[here], fn[here], fs[here], fu[here], fd[here]
        for c in range(3):
            u = src[c, here]
            total = (
                (sp[c, here] + f_e * src[c, after] + f_w * src[c, before])
                + (f_n * y_up(u) + f_s * y_dn(u))
                + (f_u * z_up(u) + f_d * z_dn(u))
            )
            yield c, u, total

    def sweep(src, dst, lo, n):
        here = pl.ds(lo, n)
        weight = ww[here]
        for c, u, total in flow(src, lo, n):
            dst[c, here] = (1.0 - OMEGA) * u + weight * total

    def restrict(lo, n):
        here = pl.ds(lo, n)
        diag, v_edge = dd[here], ve[here]
        half = n // 2
        pairs = pl.ds((lo - M) * 4, half * 8)
        for c, u, total in flow(u3, lo, n):
            res = (total - diag * u).reshape(half, 2, 8, 128)
            res = res[:, 0] + res[:, 1]
            res = res + y_up(res)
            rs[c, pairs] = res.reshape(half * 8, 128)
            flux = (v_edge * (u - gv[c, here])).reshape(half, 2, 8, 128)
            fl[c, pairs] = (flux[:, 0] + flux[:, 1]).reshape(half * 8, 128)

    def means(chunk):
        base, rows, pieces = chunk
        for c in range(3):
            for at, tile, count in pieces:
                for q in range(4):
                    if tile < 32:
                        piece = rs[c, pl.ds(tile * 8 + 2 * q, count, stride=8), :] * 0.125
                    else:
                        fr, yy, sign = (tile - 32, 0, 0.25) if tile < 40 else (tile - 40, 7, -0.25)
                        piece = fl[c, pl.ds(fr * 32 + q * 8 + yy, count, stride=32), :] * sign
                    lhs[pl.ds(c * rows + at, count), pl.ds(q * 128, 128)] = piece
        full = lhs[pl.ds(0, 3 * rows), :]
        high = full.astype(jnp.bfloat16)
        low = (full - high.astype(F32)).astype(jnp.bfloat16)
        m = mat[...]
        out = jnp.dot(high, m, preferred_element_type=F32) + jnp.dot(
            low, m, preferred_element_type=F32
        )
        return out[:, :128] * mask0, out[:, 128:] * mask1

    def main_copy(k, which):
        base, rows, _ = MAIN[k]
        part = pl.ds(base, 3 * rows)

        def held(m8):
            return main_hbm.at[2 * m8, :, part]

        mine = own.at[:, part]
        source, at, target = {
            "x": (mine, 2 * 1, (0, 1, 0)),
            "own_up": (mine, 2 * 6, (1, 0, 0)),
            "own_down": (mine, 2 * 2, (3, 0, 0)),
            "x_up": (held(1), 2 * 7, (1, 0, 0)),
            "x_down": (held(1), 2 * 3, (3, 0, 0)),
            "far_own": (held(6), 2 * 4, (1, 0, 0)),
            "far_x": (held(3), 2 * 5, (3, 0, 0)),
            "s0": (mine, 1, (0, 0, 1)),
            **{f"s{m8}": (held(m8), 2 * m8 + 1, (0, 0, 1)) for m8 in range(1, 8)},
        }[which]
        index = KINDS.index(which)
        return pltpu.make_async_remote_copy(
            src_ref=source, dst_ref=main_hbm.at[at, :, part],
            send_sem=main_send.at[k, index], recv_sem=main_recv.at[k, index],
            device_id=(g, wide_at(*target)), device_id_type=MESH,
        )

    ARRIVALS = (
        ("x", ("x_up", "x_down", "s1")),
        ("own_up", ("far_own", "s6")),
        ("own_down", ("s2",)),
        ("x_down", ("far_x", "s3")),
        ("x_up", ("s7",)),
        ("far_own", ("s4",)),
        ("far_x", ("s5",)),
    )
    KINDS = [name for name, _ in ARRIVALS] + [f"s{m8}" for m8 in range(8)]

    def own_copy(k):
        base, rows, _ = MAIN[k]
        part = pl.ds(base, 3 * rows)
        return pltpu.make_async_copy(own.at[:, part], main_hbm.at[0, :, part], out_sem.at[3 + k])

    def send_main(k):
        base, rows, _ = MAIN[k]
        p0, p1 = means(MAIN[k])
        own[0, pl.ds(base, 3 * rows), :] = p0
        own[1, pl.ds(base, 3 * rows), :] = p1
        for which in ("x", "own_up", "own_down", "s0"):
            main_copy(k, which).start()
        own_copy(k).start()

    def pass_on(k, *arrivals):
        for name, then in ARRIVALS:
            if name in arrivals:
                main_copy(k, name).wait_recv()
                for which in then:
                    main_copy(k, which).start()

    def edge_copy(off):
        dy, fx, fc = off
        index = slot_of(*off)
        return pltpu.make_async_remote_copy(
            src_ref=slots.at[index], dst_ref=edge_hbm.at[slot_of(-dy, fx, fc)],
            send_sem=edge_send.at[index], recv_sem=edge_recv.at[slot_of(-dy, fx, fc)],
            device_id=(g, wide_at(*off)), device_id_type=MESH,
        )

    def label_copy(off):
        dy, fx, fc = off
        return pltpu.make_async_remote_copy(
            src_ref=lab, dst_ref=labels_hbm.at[slot_of(-dy, fx, fc)],
            send_sem=lab_send.at[slot_of(*off)], recv_sem=lab_recv.at[slot_of(-dy, fx, fc)],
            device_id=(g, wide_at(*off)), device_id_type=MESH,
        )

    halos = []
    for side, (other, src, dst, row_x, from_sp, to_sp) in enumerate(
        ((up, NX - M, 0, NX - 1, M + NX - 3, 1), (down, 0, M + NX, 0, M, M + NX))
    ):
        pairs = (
            (stress_hbm.at[pl.ds(0, 1), row_x], sx.at[side, pl.ds(0, 1)]),
            (stress_hbm.at[pl.ds(3, 2), row_x], sx.at[side, pl.ds(1, 2)]),
            (visc_hbm.at[pl.ds(src, M)], vi.at[pl.ds(dst, M)]),
            (vel_hbm.at[:, pl.ds(src, M)], u0.at[:, pl.ds(dst, M)]),
            (sp.at[:, pl.ds(from_sp, 3)], sp.at[:, pl.ds(to_sp, 3)]),
        )
        for i, (s, t) in enumerate(pairs):
            halos.append(
                pltpu.make_async_remote_copy(
                    src_ref=s, dst_ref=t,
                    send_sem=halo_send.at[side, i], recv_sem=halo_recv.at[side, i],
                    device_id=(other, wd), device_id_type=MESH,
                )
            )

    for copy in loads:
        copy.wait()
    force(M, 4)
    force(M + NX - 4, 4)
    lane = lax.broadcasted_iota(jnp.int32, (1, 128), 1)
    lab[...] = jnp.where(lane == 0, owner_ref[0, 0], owner_ref[0, 1])
    mask0 = mask_ref[0, 0].astype(F32)
    mask1 = mask_ref[0, 1].astype(F32)
    target0 = owner_ref[0, 0] // CP_DEV
    target1 = owner_ref[0, 1] // CP_DEV

    pl.semaphore_wait(barrier, len(others) + 2)
    for copy in halos:
        copy.start()

    faces(5, 18)
    force(8, 15)
    sweep(u0, u1, 5, 18)
    sweep(u1, u2, 6, 16)
    sweep(u2, u3, 7, 14)
    restrict(8, 12)
    send_main(0)
    for off in others:
        label_copy(off).start()
    own_label = pltpu.make_async_copy(lab, labels_hbm.at[0], out_sem.at[1])
    own_label.start()
    faces(23, 24)
    force(23, 24)
    sweep(u0, u1, 23, 24)
    sweep(u1, u2, 22, 24)
    sweep(u2, u3, 21, 24)
    restrict(20, 24)
    send_main(1)
    faces(47, 20)
    force(47, 17)
    sweep(u0, u1, 47, 20)
    sweep(u1, u2, 46, 20)
    sweep(u2, u3, 45, 20)
    restrict(44, 20)
    send_main(2)
    pass_on(0, "x", "own_up", "own_down")
    pass_on(1, "x", "own_up", "own_down")

    for copy in halos:
        copy.wait()
    inside_low = jnp.where(g > 0, 1.0, 0.0)
    inside_high = jnp.where(g < n_grp - 1, 1.0, 0.0)
    for at, inside in ((0, inside_low), (M + NX, inside_high)):
        here = pl.ds(at, M)
        u0[:, here] = u0[:, here] * inside
        vi[here] = vi[here] * inside
    for c, comp in enumerate(DX_COMPS):
        sp[c, M] = sp[c, M] - (0.5 * inside_low) * sx[0, c]
        sp[c, M + NX - 1] = sp[c, M + NX - 1] + (0.5 * inside_high) * sx[1, c]
        sp[c, M - 1] = sp[c, M - 1] + 0.5 * st[comp, 1]
        sp[c, M + NX] = sp[c, M + NX] - 0.5 * st[comp, NX]
    faces(1, 3, inside_low)
    faces(M + NX, 3, inside_high)
    faces(M, 1)
    faces(M + NX - 1, 1)
    for src, dst, shift in ((u0, u1, 1), (u1, u2, 2), (u2, u3, 3)):
        sweep(src, dst, shift, 4)
        sweep(src, dst, EX - 4 - shift, 4)
    store = pltpu.make_async_copy(u3.at[:, pl.ds(M, NX)], newvel_hbm, out_sem.at[0])
    store.start()
    restrict(M, 4)
    restrict(M + NX - 4, 4)
    p0, p1 = means(EDGE)
    for off in others + [(0, 0, 0)]:
        t = wide_at(*off)
        s0 = jnp.where(target0 == t, 1.0, 0.0)
        s1 = jnp.where(target1 == t, 1.0, 0.0)
        slots[slot_of(*off)] = p0 * s0 + p1 * s1
        if off != (0, 0, 0):
            edge_copy(off).start()
    own_edge = pltpu.make_async_copy(slots.at[0], edge_hbm.at[0], out_sem.at[2])
    own_edge.start()

    pass_on(2, "x", "own_up", "own_down")
    for k in range(3):
        pass_on(k, "x_down", "x_up", "far_own", "far_x")
    for k in range(3):
        for which in KINDS:
            main_copy(k, which).wait_send()
        for m8 in range(8):
            main_copy(k, f"s{m8}").wait_recv()
        own_copy(k).wait()
    for off in others:
        label_copy(off).wait()
        edge_copy(off).wait()
    own_label.wait()
    own_edge.wait()
    store.wait()


def sum_kernel(labels_ref, vel_hbm, main_hbm, edge_hbm, newvel_hbm, out_ref, main, edge, main_sem, sems):
    me = lax.axis_index("wide")
    move = pltpu.make_async_copy(vel_hbm, newvel_hbm, sems.at[0])
    fetch = pltpu.make_async_copy(edge_hbm, edge, sems.at[1])
    hits = []
    for d in range(N_WIDE):
        first, second = labels_ref[d, 0, 0], labels_ref[d, 0, 1]
        hit0 = first // CP_DEV == me
        hit1 = second // CP_DEV == me
        index = jnp.where(hit0, first, second) % CP_DEV
        copy = pltpu.make_async_copy(
            main_hbm.at[d, jnp.where(hit0, 0, 1)], main.at[d], main_sem.at[d]
        )
        hits.append((hit0 | hit1, (index // 8) * 384 + index % 8, copy))

        @pl.when(hit0 | hit1)
        def _():
            copy.start()

    fetch.start()
    move.start()
    out_ref[...] = jnp.zeros_like(out_ref)
    fetch.wait()
    for d, (hit, start, copy) in enumerate(hits):

        @pl.when(hit)
        def _():
            copy.wait()
            for buffer, chunks in ((main, MAIN), (edge, (EDGE,))):
                for base, rows, pieces in chunks:
                    for c in range(3):
                        for at, tile, count in pieces:
                            where = pl.ds(start + c * 768 + tile * 8, count, stride=8)
                            out_ref[where, :] = (
                                out_ref[where, :] + buffer[d, pl.ds(base + c * rows + at, count), :]
                            )

    move.wait()


def on_device(velocity, coarse_ghost, viscosity, stress, patch_mask, coarse_owner):
    n_grp = lax.axis_size("grp")
    hbm = pl.BlockSpec(memory_space=pltpu.HBM)
    scalar_field = pltpu.VMEM((EX, 8, 128), F32)
    field = pltpu.VMEM((3, EX, 8, 128), F32)
    dma = pltpu.SemaphoreType.DMA
    operands = [
        pltpu.with_memory_space_constraint(a, pltpu.HBM)
        for a in (patch_mask, coarse_owner, velocity, coarse_ghost, viscosity, stress)
    ]
    new_velocity, main, edge, labels = pl.pallas_call(
        functools.partial(step_kernel, n_grp),
        out_shape=(
            jax.ShapeDtypeStruct((3, NX, 8, 128), F32),
            jax.ShapeDtypeStruct((N_WIDE, 2, 120, 128), F32),
            jax.ShapeDtypeStruct((N_WIDE, 24, 128), F32),
            jax.ShapeDtypeStruct((N_WIDE, 1, 128), jnp.int32),
        ),
        in_specs=[hbm] * 6,
        out_specs=(hbm,) * 4,
        scratch_shapes=[
            field, pltpu.VMEM((6, NX + 2, 8, 128), F32), pltpu.VMEM((2, 3, 8, 128), F32),
            scalar_field, pltpu.VMEM((3, NX, 2, 128), F32),
            *[scalar_field] * 9,
            field, field, field, field, field,
            pltpu.VMEM((3, 256, 128), F32), pltpu.VMEM((3, 256, 128), F32),
            pltpu.VMEM((48, 512), F32), pltpu.VMEM((512, 256), jnp.bfloat16),
            pltpu.VMEM((2, 120, 128), F32), pltpu.VMEM((N_WIDE, 24, 128), F32),
            pltpu.VMEM((1, 128), jnp.int32),
            pltpu.SMEM((1, 2), jnp.int32), pltpu.SMEM((1, 2), jnp.int32),
            dma((6,)),
            dma((2, 5)), dma((2, 5)),
            dma((N_WIDE,)), dma((N_WIDE,)), dma((N_WIDE,)), dma((N_WIDE,)),
            dma((3, 15)), dma((3, 15)),
            dma((6,)),
        ],
        compiler_params=pltpu.CompilerParams(
            collective_id=0, has_side_effects=True, vmem_limit_bytes=40 << 20
        ),
        name="smooth_and_send",
    )(*operands)
    new_velocity, coarse = pl.pallas_call(
        sum_kernel,
        out_shape=(
            jax.ShapeDtypeStruct((3, NX, 8, 128), F32),
            jax.ShapeDtypeStruct((2304, 128), F32),
        ),
        in_specs=[pl.BlockSpec(memory_space=pltpu.SMEM), hbm, hbm, hbm],
        out_specs=(hbm, pl.BlockSpec(memory_space=pltpu.VMEM)),
        scratch_shapes=[
            pltpu.VMEM((N_WIDE, 120, 128), F32), pltpu.VMEM((N_WIDE, 24, 128), F32),
            dma((N_WIDE,)), dma((2,)),
        ],
        compiler_params=pltpu.CompilerParams(vmem_limit_bytes=40 << 20),
        name="sum_on_owners",
    )(labels, new_velocity, main, edge)
    coarse = coarse.reshape(3, 2, 48, 8, 128).transpose(1, 3, 0, 2, 4)
    return new_velocity, coarse.reshape(1, CP_DEV, 3, 48 * 128)


def solution(mesh):
    in_specs = (
        P(None, "grp", "wide", None),
        P(None, "grp", "wide", None),
        P("grp", "wide", None),
        P(None, "grp", "wide", None),
        P("grp", "wide"),
        P("grp", "wide"),
    )
    out_specs = (P(None, "grp", "wide", None), P("grp", "wide", None, None))
    return jax.shard_map(
        on_device, mesh=mesh, in_specs=in_specs, out_specs=out_specs, check_vma=False
    )
```

```python
import functools

import jax
import jax.numpy as jnp
from jax import lax
from jax.experimental import pallas as pl
from jax.experimental.pallas import tpu as pltpu
from jax.sharding import PartitionSpec as P

MESH = pl.DeviceIdType.MESH
F32 = jnp.float32

NX = 64
M = 4
EX = NX + 2 * M
KAPPA = 1.0
OMEGA = 0.8
CP_DEV = 16
N_WIDE = 16
DX_COMPS = (0, 3, 4)

MAIN = (
    (0, 8, ((0, 2, 6), (6, 33, 1), (7, 41, 1))),
    (24, 16, ((0, 8, 8), (8, 16, 4), (12, 34, 2), (14, 42, 2))),
    (72, 16, ((0, 20, 8), (8, 28, 2), (10, 36, 3), (13, 44, 3))),
)
EDGE = (0, 8, ((0, 0, 2), (2, 30, 2), (4, 32, 1), (5, 39, 1), (6, 40, 1), (7, 47, 1)))


def step_kernel(
    n_grp,
    mask_hbm, owner_hbm, vel_hbm, ghost_hbm, visc_hbm, stress_hbm,
    newvel_hbm, main_hbm, edge_hbm, labels_hbm,
    u0, st, sx, vi, gh, fe, fw, fn, fs, fu, fd, ww, dd, ve, sp, gv, u1, u2, u3, rs, fl,
    lhs, mat, own, slots, lab, mask_ref, owner_ref,
    in_sem, halo_send, halo_recv, lab_send, lab_recv, edge_send, edge_recv, main_send, main_recv,
    out_sem,
):
    g = lax.axis_index("grp")
    wd = lax.axis_index("wide")
    up = lax.rem(g + 1, n_grp)
    down = lax.rem(g + n_grp - 1, n_grp)
    y, x, core = wd // 4, (wd // 2) % 2, wd % 2

    def wide_at(dy, fx, fc):
        return (
            ((y + dy) % 4) * 4
            + (1 - x if fx else x) * 2
            + (1 - core if fc else core)
        )

    others = [(dy, fx, fc) for dy in (2, 1, 3, 0) for fx in (1, 0) for fc in (0, 1)]
    others.remove((0, 0, 0))

    def slot_of(dy, fx, fc):
        return ((dy % 4) * 2 + fx) * 2 + fc

    loads = [
        pltpu.make_async_copy(visc_hbm, vi.at[pl.ds(M, NX)], in_sem.at[2]),
        pltpu.make_async_copy(stress_hbm, st.at[:, pl.ds(1, NX)], in_sem.at[1]),
        pltpu.make_async_copy(vel_hbm, u0.at[:, pl.ds(M, NX)], in_sem.at[0]),
        pltpu.make_async_copy(ghost_hbm, gh, in_sem.at[3]),
        pltpu.make_async_copy(owner_hbm, owner_ref, in_sem.at[4]),
        pltpu.make_async_copy(mask_hbm, mask_ref, in_sem.at[5]),
    ]
    for copy in loads:
        copy.start()

    barrier = pltpu.get_barrier_semaphore()
    for other in (up, down):
        pl.semaphore_signal(barrier, inc=1, device_id=(other, wd), device_id_type=MESH)
    for off in others:
        pl.semaphore_signal(barrier, inc=1, device_id=(g, wide_at(*off)), device_id_type=MESH)

    row = lax.broadcasted_iota(jnp.int32, (512, 256), 0)
    col = lax.broadcasted_iota(jnp.int32, (512, 256), 1)
    same_q = lax.shift_right_logical(row, 7) == (lax.shift_right_logical(col, 5) & 3)
    z_pair = lax.shift_right_logical(row & 127, 1)
    z_want = lax.shift_right_logical(col, 7) * 32 + (col & 31)
    mat[...] = jnp.where(same_q & (z_pair == z_want), 1.0, 0.0).astype(jnp.bfloat16)
    for comp in DX_COMPS:
        st[comp, 0] = jnp.zeros((8, 128), F32)
        st[comp, NX + 1] = jnp.zeros((8, 128), F32)

    ypos = lax.broadcasted_iota(jnp.int32, (1, 8, 128), 1)
    not_last = ypos < 7
    not_first = ypos > 0

    def y_up(a):
        return pltpu.roll(a, 7, 1)

    def y_dn(a):
        return pltpu.roll(a, 1, 1)

    def z_up(a):
        return pltpu.roll(a, 127, 2)

    def z_dn(a):
        return pltpu.roll(a, 1, 2)

    def faces(lo, n, inside=None):
        here, after, before = pl.ds(lo, n), pl.ds(lo + 1, n), pl.ds(lo - 1, n)
        v = vi[here]
        f_e = 0.5 * (v + vi[after])
        f_w = 0.5 * (v + vi[before])
        f_n = jnp.where(not_last, 0.5 * (v + y_up(v)), 0.0)
        f_s = y_dn(f_n)
        f_u = 0.5 * (v + z_up(v))
        f_d = z_dn(f_u)
        v_edge = jnp.where(not_last & not_first, 0.0, v)
        diag = KAPPA + f_e + f_w + f_n + f_s + f_u + f_d + v_edge
        weight = OMEGA / diag
        if inside is not None:
            weight = weight * inside
        fe[here], fw[here], fn[here], fs[here], fu[here], fd[here] = f_e, f_w, f_n, f_s, f_u, f_d
        ww[here], dd[here] = weight, diag

    def force(lo, n):
        here, own_rows = pl.ds(lo, n), pl.ds(lo - M, n)
        mid, after, before = pl.ds(lo - 3, n), pl.ds(lo - 2, n), pl.ds(lo - 4, n)
        v_edge = jnp.where(not_last & not_first, 0.0, vi[here])
        ve[here] = v_edge

        def d_x(c):
            return st[c, after] - st[c, before]

        def d_y(a):
            return jnp.where(not_last, y_up(a), 0.0) - jnp.where(not_first, y_dn(a), 0.0)

        def d_z(a):
            return z_up(a) - z_dn(a)

        sxy, sxz, syz = st[3, mid], st[4, mid], st[5, mid]
        slopes = (
            d_x(0) + d_y(sxy) + d_z(sxz),
            d_x(3) + d_y(st[1, mid]) + d_z(syz),
            d_x(4) + d_y(syz) + d_z(st[2, mid]),
        )
        for c in range(3):
            low = jnp.broadcast_to(gh[c, own_rows, 0:1, :], (n, 8, 128))
            high = jnp.broadcast_to(gh[c, own_rows, 1:2, :], (n, 8, 128))
            edge = jnp.where(not_first, jnp.where(not_last, 0.0, high), low)
            gv[c, here] = edge
            sp[c, here] = KAPPA * u0[c, here] + 0.5 * slopes[c] + v_edge * edge

    def flow(src, lo, n):
        here, after, before = pl.ds(lo, n), pl.ds(lo + 1, n), pl.ds(lo - 1, n)
        f_e, f_w, f_n, f_s, f_u, f_d = fe[here], fw[here], fn[here], fs[here], fu[here], fd[here]
        for c in range(3):
            u = src[c, here]
            total = (
                (sp[c, here] + f_e * src[c, after] + f_w * src[c, before])
                + (f_n * y_up(u) + f_s * y_dn(u))
                + (f_u * z_up(u) + f_d * z_dn(u))
            )
            yield c, u, total

    def sweep(src, dst, lo, n):
        here = pl.ds(lo, n)
        weight = ww[here]
        for c, u, total in flow(src, lo, n):
            dst[c, here] = (1.0 - OMEGA) * u + weight * total

    def restrict(lo, n):
        here = pl.ds(lo, n)
        diag, v_edge = dd[here], ve[here]
        half = n // 2
        pairs = pl.ds((lo - M) * 4, half * 8)
        for c, u, total in flow(u3, lo, n):
            res = (total - diag * u).reshape(half, 2, 8, 128)
            res = res[:, 0] + res[:, 1]
            res = res + y_up(res)
            rs[c, pairs] = res.reshape(half * 8, 128)
            flux = (v_edge * (u - gv[c, here])).reshape(half, 2, 8, 128)
            fl[c, pairs] = (flux[:, 0] + flux[:, 1]).reshape(half * 8, 128)

    def means(chunk):
        base, rows, pieces = chunk
        for c in range(3):
            for at, tile, count in pieces:
                for q in range(4):
                    if tile < 32:
                        piece = rs[c, pl.ds(tile * 8 + 2 * q, count, stride=8), :] * 0.125
                    else:
                        fr, yy, sign = (tile - 32, 0, 0.25) if tile < 40 else (tile - 40, 7, -0.25)
                        piece = fl[c, pl.ds(fr * 32 + q * 8 + yy, count, stride=32), :] * sign
                    lhs[pl.ds(c * rows + at, count), pl.ds(q * 128, 128)] = piece
        full = lhs[pl.ds(0, 3 * rows), :]
        high = full.astype(jnp.bfloat16)
        low = (full - high.astype(F32)).astype(jnp.bfloat16)
        m = mat[...]
        out = jnp.dot(high, m, preferred_element_type=F32) + jnp.dot(
            low, m, preferred_element_type=F32
        )
        return out[:, :128] * mask0, out[:, 128:] * mask1

    def main_copy(k, which):
        base, rows, _ = MAIN[k]
        part = pl.ds(base, 3 * rows)

        def held(m8):
            return main_hbm.at[2 * m8, :, part]

        mine = own.at[:, part]
        source, at, target = {
            "x": (mine, 2 * 1, (0, 1, 0)),
            "own_up": (mine, 2 * 6, (1, 0, 0)),
            "own_down": (mine, 2 * 2, (3, 0, 0)),
            "x_up": (held(1), 2 * 7, (1, 0, 0)),
            "x_down": (held(1), 2 * 3, (3, 0, 0)),
            "far_own": (held(6), 2 * 4, (1, 0, 0)),
            "far_x": (held(3), 2 * 5, (3, 0, 0)),
            "s0": (mine, 1, (0, 0, 1)),
            **{f"s{m8}": (held(m8), 2 * m8 + 1, (0, 0, 1)) for m8 in range(1, 8)},
        }[which]
        index = KINDS.index(which)
        return pltpu.make_async_remote_copy(
            src_ref=source, dst_ref=main_hbm.at[at, :, part],
            send_sem=main_send.at[k, index], recv_sem=main_recv.at[k, index],
            device_id=(g, wide_at(*target)), device_id_type=MESH,
        )

    ARRIVALS = (
        ("x", ("x_up", "x_down", "s1")),
        ("own_up", ("far_own", "s6")),
        ("own_down", ("s2",)),
        ("x_down", ("far_x", "s3")),
        ("x_up", ("s7",)),
        ("far_own", ("s4",)),
        ("far_x", ("s5",)),
    )
    KINDS = [name for name, _ in ARRIVALS] + [f"s{m8}" for m8 in range(8)]

    def own_copy(k):
        base, rows, _ = MAIN[k]
        part = pl.ds(base, 3 * rows)
        return pltpu.make_async_copy(own.at[:, part], main_hbm.at[0, :, part], out_sem.at[3 + k])

    def send_main(k):
        base, rows, _ = MAIN[k]
        p0, p1 = means(MAIN[k])
        own[0, pl.ds(base, 3 * rows), :] = p0
        own[1, pl.ds(base, 3 * rows), :] = p1
        for which in ("x", "own_up", "own_down", "s0"):
            main_copy(k, which).start()
        own_copy(k).start()

    def pass_on(k, *arrivals):
        for name, then in ARRIVALS:
            if name in arrivals:
                main_copy(k, name).wait_recv()
                for which in then:
                    main_copy(k, which).start()

    def edge_copy(off):
        dy, fx, fc = off
        index = slot_of(*off)
        return pltpu.make_async_remote_copy(
            src_ref=slots.at[index], dst_ref=edge_hbm.at[slot_of(-dy, fx, fc)],
            send_sem=edge_send.at[index], recv_sem=edge_recv.at[slot_of(-dy, fx, fc)],
            device_id=(g, wide_at(*off)), device_id_type=MESH,
        )

    def label_copy(off):
        dy, fx, fc = off
        return pltpu.make_async_remote_copy(
            src_ref=lab, dst_ref=labels_hbm.at[slot_of(-dy, fx, fc)],
            send_sem=lab_send.at[slot_of(*off)], recv_sem=lab_recv.at[slot_of(-dy, fx, fc)],
            device_id=(g, wide_at(*off)), device_id_type=MESH,
        )

    halos = []
    for side, (other, row_x, visc_at, vel_at, from_sp, from_u1, to) in enumerate(
        (
            (up, NX - 1, NX - 3, NX - 2, M + NX - 2, M + NX - 3, (1, 2, 2, 1)),
            (down, 0, 0, 0, M, M + 1, (M + NX, M + NX, M + NX, M + NX + 1)),
        )
    ):
        to_visc, to_vel, to_sp, to_u1 = to
        pairs = (
            (u1.at[:, pl.ds(from_u1, 2)], u1.at[:, pl.ds(to_u1, 2)]),
            (stress_hbm.at[pl.ds(0, 1), row_x], sx.at[side, pl.ds(0, 1)]),
            (stress_hbm.at[pl.ds(3, 2), row_x], sx.at[side, pl.ds(1, 2)]),
            (visc_hbm.at[pl.ds(visc_at, 3)], vi.at[pl.ds(to_visc, 3)]),
            (vel_hbm.at[:, pl.ds(vel_at, 2)], u0.at[:, pl.ds(to_vel, 2)]),
            (sp.at[:, pl.ds(from_sp, 2)], sp.at[:, pl.ds(to_sp, 2)]),
        )
        for i, (s, t) in enumerate(pairs):
            halos.append(
                pltpu.make_async_remote_copy(
                    src_ref=s, dst_ref=t,
                    send_sem=halo_send.at[side, i], recv_sem=halo_recv.at[side, i],
                    device_id=(other, wd), device_id_type=MESH,
                )
            )

    for copy in loads:
        copy.wait()
    force(M, 4)
    force(M + NX - 4, 4)
    lane = lax.broadcasted_iota(jnp.int32, (1, 128), 1)
    lab[...] = jnp.where(lane == 0, owner_ref[0, 0], owner_ref[0, 1])
    mask0 = mask_ref[0, 0].astype(F32)
    mask1 = mask_ref[0, 1].astype(F32)
    target0 = owner_ref[0, 0] // CP_DEV
    target1 = owner_ref[0, 1] // CP_DEV

    pl.semaphore_wait(barrier, len(others) + 2)
    for i, copy in enumerate(halos):
        if i % 6:
            copy.start()
    faces(5, 2)
    faces(M + NX - 3, 2)
    sweep(u0, u1, 5, 2)
    sweep(u0, u1, M + NX - 3, 2)
    halos[0].start()
    halos[6].start()

    faces(7, 16)
    force(8, 15)
    sweep(u0, u1, 7, 16)
    sweep(u1, u2, 6, 16)
    sweep(u2, u3, 7, 14)
    restrict(8, 12)
    send_main(0)
    own_label = pltpu.make_async_copy(lab, labels_hbm.at[0], out_sem.at[1])
    own_label.start()
    faces(23, 24)
    force(23, 24)
    sweep(u0, u1, 23, 24)
    sweep(u1, u2, 22, 24)
    sweep(u2, u3, 21, 24)
    restrict(20, 24)
    send_main(1)
    faces(47, 18)
    force(47, 17)
    sweep(u0, u1, 47, 18)
    sweep(u1, u2, 46, 20)
    sweep(u2, u3, 45, 20)
    restrict(44, 20)
    send_main(2)
    pass_on(0, "x", "own_up", "own_down")
    pass_on(1, "x", "own_up", "own_down")

    for copy in halos:
        copy.wait()
    inside_low = jnp.where(g > 0, 1.0, 0.0)
    inside_high = jnp.where(g < n_grp - 1, 1.0, 0.0)
    for at, swept, inside in ((1, 1, inside_low), (M + NX, M + NX + 1, inside_high)):
        here = pl.ds(swept, 2)
        u1[:, here] = u1[:, here] * inside
        here = pl.ds(2 if at == 1 else at, 2)
        u0[:, here] = u0[:, here] * inside
        here = pl.ds(at, 3)
        vi[here] = vi[here] * inside
    for c, comp in enumerate(DX_COMPS):
        sp[c, M] = sp[c, M] - (0.5 * inside_low) * sx[0, c]
        sp[c, M + NX - 1] = sp[c, M + NX - 1] + (0.5 * inside_high) * sx[1, c]
        sp[c, M - 1] = sp[c, M - 1] + 0.5 * st[comp, 1]
        sp[c, M + NX] = sp[c, M + NX] - 0.5 * st[comp, NX]
    faces(2, 2, inside_low)
    faces(M + NX, 2, inside_high)
    faces(M, 1)
    faces(M + NX - 1, 1)
    sweep(u0, u1, 3, 2)
    sweep(u0, u1, M + NX - 1, 2)
    for src, dst, shift in ((u1, u2, 2), (u2, u3, 3)):
        sweep(src, dst, shift, 4)
        sweep(src, dst, EX - 4 - shift, 4)
    store = pltpu.make_async_copy(u3.at[:, pl.ds(M, NX)], newvel_hbm, out_sem.at[0])
    store.start()
    restrict(M, 4)
    restrict(M + NX - 4, 4)
    p0, p1 = means(EDGE)
    for off in others + [(0, 0, 0)]:
        t = wide_at(*off)
        s0 = jnp.where(target0 == t, 1.0, 0.0)
        s1 = jnp.where(target1 == t, 1.0, 0.0)
        slots[slot_of(*off)] = p0 * s0 + p1 * s1
        if off != (0, 0, 0):
            edge_copy(off).start()
    own_edge = pltpu.make_async_copy(slots.at[0], edge_hbm.at[0], out_sem.at[2])
    own_edge.start()
    for off in others:
        label_copy(off).start()

    pass_on(2, "x", "own_up", "own_down")
    for k in range(3):
        pass_on(k, "x_down", "x_up")
    for k in range(3):
        pass_on(k, "far_own", "far_x")
    for k in range(3):
        for which in KINDS:
            main_copy(k, which).wait_send()
        for m8 in range(8):
            main_copy(k, f"s{m8}").wait_recv()
        own_copy(k).wait()
    for off in others:
        label_copy(off).wait()
        edge_copy(off).wait()
    own_label.wait()
    own_edge.wait()
    store.wait()


def sum_kernel(labels_ref, vel_hbm, main, edge, newvel_hbm, out_hbm, total, laid_out, sems):
    me = lax.axis_index("wide")
    move = pltpu.make_async_copy(vel_hbm, newvel_hbm, sems.at[3])
    move.start()
    total[...] = jnp.zeros_like(total)
    for d in range(N_WIDE):
        first, second = labels_ref[d, 0, 0], labels_ref[d, 0, 1]
        hit0 = first // CP_DEV == me
        hit1 = second // CP_DEV == me
        index = jnp.where(hit0, first, second) % CP_DEV
        patch = jnp.where(hit0, 0, 1)

        @pl.when(hit0 | hit1)
        def _():
            total[index, :120] = total[index, :120] + main[d, patch]
            total[index, 120:] = total[index, 120:] + edge[d]

    stores = []
    for c in range(3):
        for k in range(CP_DEV):
            start = c * 768 + (k // 8) * 384 + k % 8
            for first_row, chunks in ((0, MAIN), (120, (EDGE,))):
                for base, rows, pieces in chunks:
                    for at, tile, count in pieces:
                        laid_out[pl.ds(start + tile * 8, count, stride=8), :] = total[
                            k, pl.ds(first_row + base + c * rows + at, count), :
                        ]
        part = pl.ds(c * 768, 768)
        stores.append(pltpu.make_async_copy(laid_out.at[part], out_hbm.at[part], sems.at[c]))
        stores[-1].start()
    for store in stores:
        store.wait()
    move.wait()


def on_device(velocity, coarse_ghost, viscosity, stress, patch_mask, coarse_owner):
    n_grp = lax.axis_size("grp")
    hbm = pl.BlockSpec(memory_space=pltpu.HBM)
    vmem = pl.BlockSpec(memory_space=pltpu.VMEM)
    scalar_field = pltpu.VMEM((EX, 8, 128), F32)
    field = pltpu.VMEM((3, EX, 8, 128), F32)
    dma = pltpu.SemaphoreType.DMA
    operands = [
        pltpu.with_memory_space_constraint(a, pltpu.HBM)
        for a in (patch_mask, coarse_owner, velocity, coarse_ghost, viscosity, stress)
    ]
    new_velocity, main, edge, labels = pl.pallas_call(
        functools.partial(step_kernel, n_grp),
        out_shape=(
            jax.ShapeDtypeStruct((3, NX, 8, 128), F32),
            jax.ShapeDtypeStruct((N_WIDE, 2, 120, 128), F32),
            jax.ShapeDtypeStruct((N_WIDE, 24, 128), F32),
            jax.ShapeDtypeStruct((N_WIDE, 1, 128), jnp.int32),
        ),
        in_specs=[hbm] * 6,
        out_specs=(hbm,) * 4,
        scratch_shapes=[
            field, pltpu.VMEM((6, NX + 2, 8, 128), F32), pltpu.VMEM((2, 3, 8, 128), F32),
            scalar_field, pltpu.VMEM((3, NX, 2, 128), F32),
            *[scalar_field] * 9,
            field, field, field, field, field,
            pltpu.VMEM((3, 256, 128), F32), pltpu.VMEM((3, 256, 128), F32),
            pltpu.VMEM((48, 512), F32), pltpu.VMEM((512, 256), jnp.bfloat16),
            pltpu.VMEM((2, 120, 128), F32), pltpu.VMEM((N_WIDE, 24, 128), F32),
            pltpu.VMEM((1, 128), jnp.int32),
            pltpu.SMEM((1, 2), jnp.int32), pltpu.SMEM((1, 2), jnp.int32),
            dma((6,)),
            dma((2, 6)), dma((2, 6)),
            dma((N_WIDE,)), dma((N_WIDE,)), dma((N_WIDE,)), dma((N_WIDE,)),
            dma((3, 15)), dma((3, 15)),
            dma((6,)),
        ],
        compiler_params=pltpu.CompilerParams(
            collective_id=0, has_side_effects=True, vmem_limit_bytes=40 << 20
        ),
        name="smooth_and_send",
    )(*operands)
    new_velocity, coarse = pl.pallas_call(
        sum_kernel,
        out_shape=(
            jax.ShapeDtypeStruct((3, NX, 8, 128), F32),
            jax.ShapeDtypeStruct((2304, 128), F32),
        ),
        in_specs=[pl.BlockSpec(memory_space=pltpu.SMEM), hbm, vmem, vmem],
        out_specs=(hbm, hbm),
        scratch_shapes=[
            pltpu.VMEM((CP_DEV, 144, 128), F32), pltpu.VMEM((2304, 128), F32), dma((4,)),
        ],
        compiler_params=pltpu.CompilerParams(vmem_limit_bytes=40 << 20),
        name="sum_on_owners",
    )(labels, new_velocity, main, edge)
    coarse = coarse.reshape(3, 2, 48, 8, 128).transpose(1, 3, 0, 2, 4)
    return new_velocity, coarse.reshape(1, CP_DEV, 3, 48 * 128)


def solution(mesh):
    in_specs = (
        P(None, "grp", "wide", None),
        P(None, "grp", "wide", None),
        P("grp", "wide", None),
        P(None, "grp", "wide", None),
        P("grp", "wide"),
        P("grp", "wide"),
    )
    out_specs = (P(None, "grp", "wide", None), P("grp", "wide", None, None))
    return jax.shard_map(
        on_device, mesh=mesh, in_specs=in_specs, out_specs=out_specs, check_vma=False
    )
```

```python
import functools

import jax
import jax.numpy as jnp
from jax import lax
from jax.experimental import pallas as pl
from jax.experimental.pallas import tpu as pltpu
from jax.sharding import PartitionSpec as P

MESH = pl.DeviceIdType.MESH
F32 = jnp.float32

NX = 64
M = 4
EX = NX + 2 * M
KAPPA = 1.0
OMEGA = 0.8
CP_DEV = 16
N_WIDE = 16
DX_COMPS = (0, 3, 4)

MAIN = (
    (0, 16, ((0, 2, 8), (8, 10, 4), (12, 33, 2), (14, 41, 2))),
    (48, 16, ((0, 14, 8), (8, 22, 2), (10, 35, 3), (13, 43, 3))),
    (96, 8, ((0, 24, 6), (6, 38, 1), (7, 46, 1))),
)
EDGE = (0, 8, ((0, 0, 2), (2, 30, 2), (4, 32, 1), (5, 39, 1), (6, 40, 1), (7, 47, 1)))


def step_kernel(
    n_grp,
    mask_hbm, owner_hbm, vel_hbm, ghost_hbm, visc_hbm, stress_hbm,
    newvel_hbm, main_hbm, edge_hbm, labels_hbm,
    u0, st, sx, vi, gh, fe, fw, fn, fs, fu, fd, ww, dd, ve, sp, gv, u1, u2, u3, rs, fl,
    lhs, mat, own, slots, lab, mask_ref, owner_ref,
    in_sem, halo_send, halo_recv, lab_send, lab_recv, edge_send, edge_recv, main_send, main_recv,
    out_sem,
):
    g = lax.axis_index("grp")
    wd = lax.axis_index("wide")
    up = lax.rem(g + 1, n_grp)
    down = lax.rem(g + n_grp - 1, n_grp)
    y, x, core = wd // 4, (wd // 2) % 2, wd % 2

    def wide_at(dy, fx, fc):
        return (
            ((y + dy) % 4) * 4
            + (1 - x if fx else x) * 2
            + (1 - core if fc else core)
        )

    others = [(dy, fx, fc) for dy in (2, 1, 3, 0) for fx in (1, 0) for fc in (0, 1)]
    others.remove((0, 0, 0))

    def slot_of(dy, fx, fc):
        return ((dy % 4) * 2 + fx) * 2 + fc

    loads = [
        pltpu.make_async_copy(visc_hbm, vi.at[pl.ds(M, NX)], in_sem.at[2]),
        pltpu.make_async_copy(stress_hbm, st.at[:, pl.ds(1, NX)], in_sem.at[1]),
        pltpu.make_async_copy(vel_hbm, u0.at[:, pl.ds(M, NX)], in_sem.at[0]),
        pltpu.make_async_copy(ghost_hbm, gh, in_sem.at[3]),
        pltpu.make_async_copy(owner_hbm, owner_ref, in_sem.at[4]),
        pltpu.make_async_copy(mask_hbm, mask_ref, in_sem.at[5]),
    ]
    for copy in loads:
        copy.start()

    barrier = pltpu.get_barrier_semaphore()
    for other in (up, down):
        pl.semaphore_signal(barrier, inc=1, device_id=(other, wd), device_id_type=MESH)
    for off in others:
        pl.semaphore_signal(barrier, inc=1, device_id=(g, wide_at(*off)), device_id_type=MESH)

    row = lax.broadcasted_iota(jnp.int32, (512, 256), 0)
    col = lax.broadcasted_iota(jnp.int32, (512, 256), 1)
    same_q = lax.shift_right_logical(row, 7) == (lax.shift_right_logical(col, 5) & 3)
    z_pair = lax.shift_right_logical(row & 127, 1)
    z_want = lax.shift_right_logical(col, 7) * 32 + (col & 31)
    mat[...] = jnp.where(same_q & (z_pair == z_want), 1.0, 0.0).astype(jnp.bfloat16)
    for comp in DX_COMPS:
        st[comp, 0] = jnp.zeros((8, 128), F32)
        st[comp, NX + 1] = jnp.zeros((8, 128), F32)

    ypos = lax.broadcasted_iota(jnp.int32, (1, 8, 128), 1)
    not_last = ypos < 7
    not_first = ypos > 0

    def y_up(a):
        return pltpu.roll(a, 7, 1)

    def y_dn(a):
        return pltpu.roll(a, 1, 1)

    def z_up(a):
        return pltpu.roll(a, 127, 2)

    def z_dn(a):
        return pltpu.roll(a, 1, 2)

    def faces(lo, n, inside=None):
        here, after, before = pl.ds(lo, n), pl.ds(lo + 1, n), pl.ds(lo - 1, n)
        v = vi[here]
        f_e = 0.5 * (v + vi[after])
        f_w = 0.5 * (v + vi[before])
        f_n = jnp.where(not_last, 0.5 * (v + y_up(v)), 0.0)
        f_s = y_dn(f_n)
        f_u = 0.5 * (v + z_up(v))
        f_d = z_dn(f_u)
        v_edge = jnp.where(not_last & not_first, 0.0, v)
        diag = KAPPA + f_e + f_w + f_n + f_s + f_u + f_d + v_edge
        weight = OMEGA / diag
        if inside is not None:
            weight = weight * inside
        fe[here], fw[here], fn[here], fs[here], fu[here], fd[here] = f_e, f_w, f_n, f_s, f_u, f_d
        ww[here], dd[here] = weight, diag

    def force(lo, n):
        here, own_rows = pl.ds(lo, n), pl.ds(lo - M, n)
        mid, after, before = pl.ds(lo - 3, n), pl.ds(lo - 2, n), pl.ds(lo - 4, n)
        v_edge = jnp.where(not_last & not_first, 0.0, vi[here])
        ve[here] = v_edge

        def d_x(c):
            return st[c, after] - st[c, before]

        def d_y(a):
            return jnp.where(not_last, y_up(a), 0.0) - jnp.where(not_first, y_dn(a), 0.0)

        def d_z(a):
            return z_up(a) - z_dn(a)

        sxy, sxz, syz = st[3, mid], st[4, mid], st[5, mid]
        slopes = (
            d_x(0) + d_y(sxy) + d_z(sxz),
            d_x(3) + d_y(st[1, mid]) + d_z(syz),
            d_x(4) + d_y(syz) + d_z(st[2, mid]),
        )
        for c in range(3):
            low = jnp.broadcast_to(gh[c, own_rows, 0:1, :], (n, 8, 128))
            high = jnp.broadcast_to(gh[c, own_rows, 1:2, :], (n, 8, 128))
            edge = jnp.where(not_first, jnp.where(not_last, 0.0, high), low)
            gv[c, here] = edge
            sp[c, here] = KAPPA * u0[c, here] + 0.5 * slopes[c] + v_edge * edge

    def flow(src, lo, n):
        here, after, before = pl.ds(lo, n), pl.ds(lo + 1, n), pl.ds(lo - 1, n)
        f_e, f_w, f_n, f_s, f_u, f_d = fe[here], fw[here], fn[here], fs[here], fu[here], fd[here]
        for c in range(3):
            u = src[c, here]
            total = (
                (sp[c, here] + f_e * src[c, after] + f_w * src[c, before])
                + (f_n * y_up(u) + f_s * y_dn(u))
                + (f_u * z_up(u) + f_d * z_dn(u))
            )
            yield c, u, total

    def sweep(src, dst, lo, n):
        here = pl.ds(lo, n)
        weight = ww[here]
        for c, u, total in flow(src, lo, n):
            dst[c, here] = (1.0 - OMEGA) * u + weight * total

    def restrict(lo, n):
        here = pl.ds(lo, n)
        diag, v_edge = dd[here], ve[here]
        half = n // 2
        pairs = pl.ds((lo - M) * 4, half * 8)
        for c, u, total in flow(u3, lo, n):
            res = (total - diag * u).reshape(half, 2, 8, 128)
            res = res[:, 0] + res[:, 1]
            res = res + y_up(res)
            rs[c, pairs] = res.reshape(half * 8, 128)
            flux = (v_edge * (u - gv[c, here])).reshape(half, 2, 8, 128)
            fl[c, pairs] = (flux[:, 0] + flux[:, 1]).reshape(half * 8, 128)

    def means(chunk):
        base, rows, pieces = chunk
        for c in range(3):
            for at, tile, count in pieces:
                for q in range(4):
                    if tile < 32:
                        piece = rs[c, pl.ds(tile * 8 + 2 * q, count, stride=8), :] * 0.125
                    else:
                        fr, yy, sign = (tile - 32, 0, 0.25) if tile < 40 else (tile - 40, 7, -0.25)
                        piece = fl[c, pl.ds(fr * 32 + q * 8 + yy, count, stride=32), :] * sign
                    lhs[pl.ds(c * rows + at, count), pl.ds(q * 128, 128)] = piece
        full = lhs[pl.ds(0, 3 * rows), :]
        high = full.astype(jnp.bfloat16)
        low = (full - high.astype(F32)).astype(jnp.bfloat16)
        m = mat[...]
        out = jnp.dot(high, m, preferred_element_type=F32) + jnp.dot(
            low, m, preferred_element_type=F32
        )
        return out[:, :128] * mask0, out[:, 128:] * mask1

    def main_copy(k, which):
        base, rows, _ = MAIN[k]
        part = pl.ds(base, 3 * rows)

        def held(m8):
            return main_hbm.at[2 * m8, :, part]

        mine = own.at[:, part]
        source, at, target = {
            "x": (mine, 2 * 1, (0, 1, 0)),
            "own_up": (mine, 2 * 6, (1, 0, 0)),
            "own_down": (mine, 2 * 2, (3, 0, 0)),
            "x_up": (held(1), 2 * 7, (1, 0, 0)),
            "x_down": (held(1), 2 * 3, (3, 0, 0)),
            "far_own": (held(6), 2 * 4, (1, 0, 0)),
            "far_x": (held(3), 2 * 5, (3, 0, 0)),
            "s0": (mine, 1, (0, 0, 1)),
            **{f"s{m8}": (held(m8), 2 * m8 + 1, (0, 0, 1)) for m8 in range(1, 8)},
        }[which]
        index = KINDS.index(which)
        return pltpu.make_async_remote_copy(
            src_ref=source, dst_ref=main_hbm.at[at, :, part],
            send_sem=main_send.at[k, index], recv_sem=main_recv.at[k, index],
            device_id=(g, wide_at(*target)), device_id_type=MESH,
        )

    ARRIVALS = (
        ("x", ("x_up", "x_down", "s1")),
        ("own_up", ("far_own", "s6")),
        ("own_down", ("s2",)),
        ("x_down", ("far_x", "s3")),
        ("x_up", ("s7",)),
        ("far_own", ("s4",)),
        ("far_x", ("s5",)),
    )
    KINDS = [name for name, _ in ARRIVALS] + [f"s{m8}" for m8 in range(8)]

    def own_copy(k):
        base, rows, _ = MAIN[k]
        part = pl.ds(base, 3 * rows)
        return pltpu.make_async_copy(own.at[:, part], main_hbm.at[0, :, part], out_sem.at[3 + k])

    def send_main(k):
        base, rows, _ = MAIN[k]
        p0, p1 = means(MAIN[k])
        own[0, pl.ds(base, 3 * rows), :] = p0
        own[1, pl.ds(base, 3 * rows), :] = p1
        for which in ("x", "own_up", "own_down", "s0"):
            main_copy(k, which).start()
        own_copy(k).start()

    def pass_on(k, *arrivals):
        for name, then in ARRIVALS:
            if name in arrivals:
                main_copy(k, name).wait_recv()
                for which in then:
                    main_copy(k, which).start()

    def edge_copy(off):
        dy, fx, fc = off
        index = slot_of(*off)
        return pltpu.make_async_remote_copy(
            src_ref=slots.at[index], dst_ref=edge_hbm.at[slot_of(-dy, fx, fc)],
            send_sem=edge_send.at[index], recv_sem=edge_recv.at[slot_of(-dy, fx, fc)],
            device_id=(g, wide_at(*off)), device_id_type=MESH,
        )

    def label_copy(off):
        dy, fx, fc = off
        return pltpu.make_async_remote_copy(
            src_ref=lab, dst_ref=labels_hbm.at[slot_of(-dy, fx, fc)],
            send_sem=lab_send.at[slot_of(*off)], recv_sem=lab_recv.at[slot_of(-dy, fx, fc)],
            device_id=(g, wide_at(*off)), device_id_type=MESH,
        )

    halos = []
    for side, (other, row_x, visc_at, vel_at, from_sp, from_u1, to) in enumerate(
        (
            (up, NX - 1, NX - 3, NX - 2, M + NX - 2, M + NX - 3, (1, 2, 2, 1)),
            (down, 0, 0, 0, M, M + 1, (M + NX, M + NX, M + NX, M + NX + 1)),
        )
    ):
        to_visc, to_vel, to_sp, to_u1 = to
        pairs = (
            (u1.at[:, pl.ds(from_u1, 2)], u1.at[:, pl.ds(to_u1, 2)]),
            (stress_hbm.at[pl.ds(0, 1), row_x], sx.at[side, pl.ds(0, 1)]),
            (stress_hbm.at[pl.ds(3, 2), row_x], sx.at[side, pl.ds(1, 2)]),
            (visc_hbm.at[pl.ds(visc_at, 3)], vi.at[pl.ds(to_visc, 3)]),
            (vel_hbm.at[:, pl.ds(vel_at, 2)], u0.at[:, pl.ds(to_vel, 2)]),
            (sp.at[:, pl.ds(from_sp, 2)], sp.at[:, pl.ds(to_sp, 2)]),
        )
        for i, (s, t) in enumerate(pairs):
            halos.append(
                pltpu.make_async_remote_copy(
                    src_ref=s, dst_ref=t,
                    send_sem=halo_send.at[side, i], recv_sem=halo_recv.at[side, i],
                    device_id=(other, wd), device_id_type=MESH,
                )
            )

    for copy in loads:
        copy.wait()
    force(M, 4)
    force(M + NX - 4, 4)
    lane = lax.broadcasted_iota(jnp.int32, (1, 128), 1)
    lab[...] = jnp.where(lane == 0, owner_ref[0, 0], owner_ref[0, 1])
    mask0 = mask_ref[0, 0].astype(F32)
    mask1 = mask_ref[0, 1].astype(F32)
    target0 = owner_ref[0, 0] // CP_DEV
    target1 = owner_ref[0, 1] // CP_DEV

    pl.semaphore_wait(barrier, len(others) + 2)
    for i, copy in enumerate(halos):
        if i % 6:
            copy.start()
    faces(5, 2)
    faces(M + NX - 3, 2)
    sweep(u0, u1, 5, 2)
    sweep(u0, u1, M + NX - 3, 2)
    halos[0].start()
    halos[6].start()

    faces(7, 28)
    force(8, 27)
    sweep(u0, u1, 7, 28)
    sweep(u1, u2, 6, 28)
    sweep(u2, u3, 7, 26)
    restrict(8, 24)
    send_main(0)
    own_label = pltpu.make_async_copy(lab, labels_hbm.at[0], out_sem.at[1])
    own_label.start()
    faces(35, 20)
    force(35, 20)
    sweep(u0, u1, 35, 20)
    sweep(u1, u2, 34, 20)
    sweep(u2, u3, 33, 20)
    restrict(32, 20)
    send_main(1)
    faces(55, 10)
    force(55, 9)
    sweep(u0, u1, 55, 10)
    sweep(u1, u2, 54, 12)
    sweep(u2, u3, 53, 12)
    restrict(52, 12)
    send_main(2)
    pass_on(0, "x", "own_up", "own_down")
    pass_on(1, "x", "own_up", "own_down")
    pass_on(2, "x", "own_up", "own_down")

    for copy in halos:
        copy.wait()
    inside_low = jnp.where(g > 0, 1.0, 0.0)
    inside_high = jnp.where(g < n_grp - 1, 1.0, 0.0)
    for at, swept, inside in ((1, 1, inside_low), (M + NX, M + NX + 1, inside_high)):
        here = pl.ds(swept, 2)
        u1[:, here] = u1[:, here] * inside
        here = pl.ds(2 if at == 1 else at, 2)
        u0[:, here] = u0[:, here] * inside
        here = pl.ds(at, 3)
        vi[here] = vi[here] * inside
    for c, comp in enumerate(DX_COMPS):
        sp[c, M] = sp[c, M] - (0.5 * inside_low) * sx[0, c]
        sp[c, M + NX - 1] = sp[c, M + NX - 1] + (0.5 * inside_high) * sx[1, c]
        sp[c, M - 1] = sp[c, M - 1] + 0.5 * st[comp, 1]
        sp[c, M + NX] = sp[c, M + NX] - 0.5 * st[comp, NX]
    faces(2, 2, inside_low)
    faces(M + NX, 2, inside_high)
    faces(M, 1)
    faces(M + NX - 1, 1)
    sweep(u0, u1, 3, 2)
    sweep(u0, u1, M + NX - 1, 2)
    for src, dst, shift in ((u1, u2, 2), (u2, u3, 3)):
        sweep(src, dst, shift, 4)
        sweep(src, dst, EX - 4 - shift, 4)
    store = pltpu.make_async_copy(u3.at[:, pl.ds(M, NX)], newvel_hbm, out_sem.at[0])
    store.start()
    restrict(M, 4)
    restrict(M + NX - 4, 4)
    p0, p1 = means(EDGE)
    for off in others + [(0, 0, 0)]:
        t = wide_at(*off)
        s0 = jnp.where(target0 == t, 1.0, 0.0)
        s1 = jnp.where(target1 == t, 1.0, 0.0)
        slots[slot_of(*off)] = p0 * s0 + p1 * s1
        if off != (0, 0, 0):
            edge_copy(off).start()
    own_edge = pltpu.make_async_copy(slots.at[0], edge_hbm.at[0], out_sem.at[2])
    own_edge.start()
    for off in others:
        label_copy(off).start()

    for k in range(3):
        pass_on(k, "x_down", "x_up")
    for k in range(3):
        pass_on(k, "far_own", "far_x")
    for k in range(3):
        for which in KINDS:
            main_copy(k, which).wait_send()
        for m8 in range(8):
            main_copy(k, f"s{m8}").wait_recv()
        own_copy(k).wait()
    for off in others:
        label_copy(off).wait()
        edge_copy(off).wait()
    own_label.wait()
    own_edge.wait()
    store.wait()


def sum_kernel(labels_ref, vel_hbm, main, edge, newvel_hbm, out_hbm, total, laid_out, sems):
    me = lax.axis_index("wide")
    move = pltpu.make_async_copy(vel_hbm, newvel_hbm, sems.at[3])
    move.start()
    total[...] = jnp.zeros_like(total)
    for d in range(N_WIDE):
        first, second = labels_ref[d, 0, 0], labels_ref[d, 0, 1]
        hit0 = first // CP_DEV == me
        hit1 = second // CP_DEV == me
        index = jnp.where(hit0, first, second) % CP_DEV
        patch = jnp.where(hit0, 0, 1)

        @pl.when(hit0 | hit1)
        def _():
            total[index, :120] = total[index, :120] + main[d, patch]
            total[index, 120:] = total[index, 120:] + edge[d]

    stores = []
    for c in range(3):
        for k in range(CP_DEV):
            start = c * 768 + (k // 8) * 384 + k % 8
            for first_row, chunks in ((0, MAIN), (120, (EDGE,))):
                for base, rows, pieces in chunks:
                    for at, tile, count in pieces:
                        laid_out[pl.ds(start + tile * 8, count, stride=8), :] = total[
                            k, pl.ds(first_row + base + c * rows + at, count), :
                        ]
        part = pl.ds(c * 768, 768)
        stores.append(pltpu.make_async_copy(laid_out.at[part], out_hbm.at[part], sems.at[c]))
        stores[-1].start()
    for store in stores:
        store.wait()
    move.wait()


def on_device(velocity, coarse_ghost, viscosity, stress, patch_mask, coarse_owner):
    n_grp = lax.axis_size("grp")
    hbm = pl.BlockSpec(memory_space=pltpu.HBM)
    vmem = pl.BlockSpec(memory_space=pltpu.VMEM)
    scalar_field = pltpu.VMEM((EX, 8, 128), F32)
    field = pltpu.VMEM((3, EX, 8, 128), F32)
    dma = pltpu.SemaphoreType.DMA
    operands = [
        pltpu.with_memory_space_constraint(a, pltpu.HBM)
        for a in (patch_mask, coarse_owner, velocity, coarse_ghost, viscosity, stress)
    ]
    new_velocity, main, edge, labels = pl.pallas_call(
        functools.partial(step_kernel, n_grp),
        out_shape=(
            jax.ShapeDtypeStruct((3, NX, 8, 128), F32),
            jax.ShapeDtypeStruct((N_WIDE, 2, 120, 128), F32),
            jax.ShapeDtypeStruct((N_WIDE, 24, 128), F32),
            jax.ShapeDtypeStruct((N_WIDE, 1, 128), jnp.int32),
        ),
        in_specs=[hbm] * 6,
        out_specs=(hbm,) * 4,
        scratch_shapes=[
            field, pltpu.VMEM((6, NX + 2, 8, 128), F32), pltpu.VMEM((2, 3, 8, 128), F32),
            scalar_field, pltpu.VMEM((3, NX, 2, 128), F32),
            *[scalar_field] * 9,
            field, field, field, field, field,
            pltpu.VMEM((3, 256, 128), F32), pltpu.VMEM((3, 256, 128), F32),
            pltpu.VMEM((48, 512), F32), pltpu.VMEM((512, 256), jnp.bfloat16),
            pltpu.VMEM((2, 120, 128), F32), pltpu.VMEM((N_WIDE, 24, 128), F32),
            pltpu.VMEM((1, 128), jnp.int32),
            pltpu.SMEM((1, 2), jnp.int32), pltpu.SMEM((1, 2), jnp.int32),
            dma((6,)),
            dma((2, 6)), dma((2, 6)),
            dma((N_WIDE,)), dma((N_WIDE,)), dma((N_WIDE,)), dma((N_WIDE,)),
            dma((3, 15)), dma((3, 15)),
            dma((6,)),
        ],
        compiler_params=pltpu.CompilerParams(
            collective_id=0, has_side_effects=True, vmem_limit_bytes=40 << 20
        ),
        name="smooth_and_send",
    )(*operands)
    new_velocity, coarse = pl.pallas_call(
        sum_kernel,
        out_shape=(
            jax.ShapeDtypeStruct((3, NX, 8, 128), F32),
            jax.ShapeDtypeStruct((2304, 128), F32),
        ),
        in_specs=[pl.BlockSpec(memory_space=pltpu.SMEM), hbm, vmem, vmem],
        out_specs=(hbm, hbm),
        scratch_shapes=[
            pltpu.VMEM((CP_DEV, 144, 128), F32), pltpu.VMEM((2304, 128), F32), dma((4,)),
        ],
        compiler_params=pltpu.CompilerParams(vmem_limit_bytes=40 << 20),
        name="sum_on_owners",
    )(labels, new_velocity, main, edge)
    coarse = coarse.reshape(3, 2, 48, 8, 128).transpose(1, 3, 0, 2, 4)
    return new_velocity, coarse.reshape(1, CP_DEV, 3, 48 * 128)


def solution(mesh):
    in_specs = (
        P(None, "grp", "wide", None),
        P(None, "grp", "wide", None),
        P("grp", "wide", None),
        P(None, "grp", "wide", None),
        P("grp", "wide"),
        P("grp", "wide"),
    )
    out_specs = (P(None, "grp", "wide", None), P("grp", "wide", None, None))
    return jax.shard_map(
        on_device, mesh=mesh, in_specs=in_specs, out_specs=out_specs, check_vma=False
    )
```

```python
import functools

import jax
import jax.numpy as jnp
from jax import lax
from jax.experimental import pallas as pl
from jax.experimental.pallas import tpu as pltpu
from jax.sharding import PartitionSpec as P

MESH = pl.DeviceIdType.MESH
F32 = jnp.float32

NX = 64
M = 4
EX = NX + 2 * M
KAPPA = 1.0
OMEGA = 0.8
CP_DEV = 16
N_WIDE = 16
DX_COMPS = (0, 3, 4)

MAIN = (
    (0, 24, ((0, 2, 8), (8, 10, 8), (16, 18, 2), (18, 33, 3), (21, 41, 3))),
    (72, 16, ((0, 20, 8), (8, 28, 2), (10, 36, 3), (13, 44, 3))),
)
EDGE = (0, 8, ((0, 0, 2), (2, 30, 2), (4, 32, 1), (5, 39, 1), (6, 40, 1), (7, 47, 1)))


def step_kernel(
    n_grp,
    mask_hbm, owner_hbm, vel_hbm, ghost_hbm, visc_hbm, stress_hbm,
    newvel_hbm, main_hbm, edge_hbm, labels_hbm,
    u0, st, sx, vi, gh, fe, fw, fn, fs, fu, fd, ww, dd, ve, sp, gv, u1, u2, u3, rs, fl,
    lhs, mat, own, slots, lab, mask_ref, owner_ref,
    in_sem, halo_send, halo_recv, lab_send, lab_recv, edge_send, edge_recv, main_send, main_recv,
    out_sem,
):
    g = lax.axis_index("grp")
    wd = lax.axis_index("wide")
    up = lax.rem(g + 1, n_grp)
    down = lax.rem(g + n_grp - 1, n_grp)
    y, x, core = wd // 4, (wd // 2) % 2, wd % 2

    def wide_at(dy, fx, fc):
        return (
            ((y + dy) % 4) * 4
            + (1 - x if fx else x) * 2
            + (1 - core if fc else core)
        )

    others = [(dy, fx, fc) for dy in (2, 1, 3, 0) for fx in (1, 0) for fc in (0, 1)]
    others.remove((0, 0, 0))

    def slot_of(dy, fx, fc):
        return ((dy % 4) * 2 + fx) * 2 + fc

    loads = [
        pltpu.make_async_copy(visc_hbm, vi.at[pl.ds(M, NX)], in_sem.at[2]),
        pltpu.make_async_copy(stress_hbm, st.at[:, pl.ds(1, NX)], in_sem.at[1]),
        pltpu.make_async_copy(vel_hbm, u0.at[:, pl.ds(M, NX)], in_sem.at[0]),
        pltpu.make_async_copy(ghost_hbm, gh, in_sem.at[3]),
        pltpu.make_async_copy(owner_hbm, owner_ref, in_sem.at[4]),
        pltpu.make_async_copy(mask_hbm, mask_ref, in_sem.at[5]),
    ]
    for copy in loads:
        copy.start()

    barrier = pltpu.get_barrier_semaphore()
    for other in (up, down):
        pl.semaphore_signal(barrier, inc=1, device_id=(other, wd), device_id_type=MESH)
    for off in others:
        pl.semaphore_signal(barrier, inc=1, device_id=(g, wide_at(*off)), device_id_type=MESH)

    row = lax.broadcasted_iota(jnp.int32, (512, 256), 0)
    col = lax.broadcasted_iota(jnp.int32, (512, 256), 1)
    same_q = lax.shift_right_logical(row, 7) == (lax.shift_right_logical(col, 5) & 3)
    z_pair = lax.shift_right_logical(row & 127, 1)
    z_want = lax.shift_right_logical(col, 7) * 32 + (col & 31)
    mat[...] = jnp.where(same_q & (z_pair == z_want), 1.0, 0.0).astype(jnp.bfloat16)
    for comp in DX_COMPS:
        st[comp, 0] = jnp.zeros((8, 128), F32)
        st[comp, NX + 1] = jnp.zeros((8, 128), F32)

    ypos = lax.broadcasted_iota(jnp.int32, (1, 8, 128), 1)
    not_last = ypos < 7
    not_first = ypos > 0

    def y_up(a):
        return pltpu.roll(a, 7, 1)

    def y_dn(a):
        return pltpu.roll(a, 1, 1)

    def z_up(a):
        return pltpu.roll(a, 127, 2)

    def z_dn(a):
        return pltpu.roll(a, 1, 2)

    def faces(lo, n, inside=None):
        here, after, before = pl.ds(lo, n), pl.ds(lo + 1, n), pl.ds(lo - 1, n)
        v = vi[here]
        f_e = 0.5 * (v + vi[after])
        f_w = 0.5 * (v + vi[before])
        f_n = jnp.where(not_last, 0.5 * (v + y_up(v)), 0.0)
        f_s = y_dn(f_n)
        f_u = 0.5 * (v + z_up(v))
        f_d = z_dn(f_u)
        v_edge = jnp.where(not_last & not_first, 0.0, v)
        diag = KAPPA + f_e + f_w + f_n + f_s + f_u + f_d + v_edge
        weight = OMEGA / diag
        if inside is not None:
            weight = weight * inside
        fe[here], fw[here], fn[here], fs[here], fu[here], fd[here] = f_e, f_w, f_n, f_s, f_u, f_d
        ww[here], dd[here] = weight, diag

    def force(lo, n):
        here, own_rows = pl.ds(lo, n), pl.ds(lo - M, n)
        mid, after, before = pl.ds(lo - 3, n), pl.ds(lo - 2, n), pl.ds(lo - 4, n)
        v_edge = jnp.where(not_last & not_first, 0.0, vi[here])
        ve[here] = v_edge

        def d_x(c):
            return st[c, after] - st[c, before]

        def d_y(a):
            return jnp.where(not_last, y_up(a), 0.0) - jnp.where(not_first, y_dn(a), 0.0)

        def d_z(a):
            return z_up(a) - z_dn(a)

        sxy, sxz, syz = st[3, mid], st[4, mid], st[5, mid]
        slopes = (
            d_x(0) + d_y(sxy) + d_z(sxz),
            d_x(3) + d_y(st[1, mid]) + d_z(syz),
            d_x(4) + d_y(syz) + d_z(st[2, mid]),
        )
        for c in range(3):
            low = jnp.broadcast_to(gh[c, own_rows, 0:1, :], (n, 8, 128))
            high = jnp.broadcast_to(gh[c, own_rows, 1:2, :], (n, 8, 128))
            edge = jnp.where(not_first, jnp.where(not_last, 0.0, high), low)
            gv[c, here] = edge
            sp[c, here] = KAPPA * u0[c, here] + 0.5 * slopes[c] + v_edge * edge

    def flow(src, lo, n):
        here, after, before = pl.ds(lo, n), pl.ds(lo + 1, n), pl.ds(lo - 1, n)
        f_e, f_w, f_n, f_s, f_u, f_d = fe[here], fw[here], fn[here], fs[here], fu[here], fd[here]
        for c in range(3):
            u = src[c, here]
            total = (
                (sp[c, here] + f_e * src[c, after] + f_w * src[c, before])
                + (f_n * y_up(u) + f_s * y_dn(u))
                + (f_u * z_up(u) + f_d * z_dn(u))
            )
            yield c, u, total

    def sweep(src, dst, lo, n):
        here = pl.ds(lo, n)
        weight = ww[here]
        for c, u, total in flow(src, lo, n):
            dst[c, here] = (1.0 - OMEGA) * u + weight * total

    def restrict(lo, n):
        here = pl.ds(lo, n)
        diag, v_edge = dd[here], ve[here]
        half = n // 2
        pairs = pl.ds((lo - M) * 4, half * 8)
        for c, u, total in flow(u3, lo, n):
            res = (total - diag * u).reshape(half, 2, 8, 128)
            res = res[:, 0] + res[:, 1]
            res = res + y_up(res)
            rs[c, pairs] = res.reshape(half * 8, 128)
            flux = (v_edge * (u - gv[c, here])).reshape(half, 2, 8, 128)
            fl[c, pairs] = (flux[:, 0] + flux[:, 1]).reshape(half * 8, 128)

    def means(chunk):
        base, rows, pieces = chunk
        for c in range(3):
            for at, tile, count in pieces:
                for q in range(4):
                    if tile < 32:
                        piece = rs[c, pl.ds(tile * 8 + 2 * q, count, stride=8), :] * 0.125
                    else:
                        fr, yy, sign = (tile - 32, 0, 0.25) if tile < 40 else (tile - 40, 7, -0.25)
                        piece = fl[c, pl.ds(fr * 32 + q * 8 + yy, count, stride=32), :] * sign
                    lhs[pl.ds(c * rows + at, count), pl.ds(q * 128, 128)] = piece
        full = lhs[pl.ds(0, 3 * rows), :]
        high = full.astype(jnp.bfloat16)
        low = (full - high.astype(F32)).astype(jnp.bfloat16)
        m = mat[...]
        out = jnp.dot(high, m, preferred_element_type=F32) + jnp.dot(
            low, m, preferred_element_type=F32
        )
        return out[:, :128] * mask0, out[:, 128:] * mask1

    def main_copy(k, which):
        base, rows, _ = MAIN[k]
        part = pl.ds(base, 3 * rows)

        def held(m8):
            return main_hbm.at[2 * m8, :, part]

        mine = own.at[:, part]
        source, at, target = {
            "x": (mine, 2 * 1, (0, 1, 0)),
            "own_up": (mine, 2 * 6, (1, 0, 0)),
            "own_down": (mine, 2 * 2, (3, 0, 0)),
            "x_up": (held(1), 2 * 7, (1, 0, 0)),
            "x_down": (held(1), 2 * 3, (3, 0, 0)),
            "far_own": (held(6), 2 * 4, (1, 0, 0)),
            "far_x": (held(3), 2 * 5, (3, 0, 0)),
            "s0": (mine, 1, (0, 0, 1)),
            **{f"s{m8}": (held(m8), 2 * m8 + 1, (0, 0, 1)) for m8 in range(1, 8)},
        }[which]
        index = KINDS.index(which)
        return pltpu.make_async_remote_copy(
            src_ref=source, dst_ref=main_hbm.at[at, :, part],
            send_sem=main_send.at[k, index], recv_sem=main_recv.at[k, index],
            device_id=(g, wide_at(*target)), device_id_type=MESH,
        )

    ARRIVALS = (
        ("x", ("x_up", "x_down", "s1")),
        ("own_up", ("far_own", "s6")),
        ("own_down", ("s2",)),
        ("x_down", ("far_x", "s3")),
        ("x_up", ("s7",)),
        ("far_own", ("s4",)),
        ("far_x", ("s5",)),
    )
    KINDS = [name for name, _ in ARRIVALS] + [f"s{m8}" for m8 in range(8)]

    def own_copy(k):
        base, rows, _ = MAIN[k]
        part = pl.ds(base, 3 * rows)
        return pltpu.make_async_copy(own.at[:, part], main_hbm.at[0, :, part], out_sem.at[3 + k])

    def send_main(k):
        base, rows, _ = MAIN[k]
        p0, p1 = means(MAIN[k])
        own[0, pl.ds(base, 3 * rows), :] = p0
        own[1, pl.ds(base, 3 * rows), :] = p1
        for which in ("x", "own_up", "own_down", "s0"):
            main_copy(k, which).start()
        own_copy(k).start()

    def pass_on(k, *arrivals):
        for name, then in ARRIVALS:
            if name in arrivals:
                main_copy(k, name).wait_recv()
                for which in then:
                    main_copy(k, which).start()

    def edge_copy(off):
        dy, fx, fc = off
        index = slot_of(*off)
        return pltpu.make_async_remote_copy(
            src_ref=slots.at[index], dst_ref=edge_hbm.at[slot_of(-dy, fx, fc)],
            send_sem=edge_send.at[index], recv_sem=edge_recv.at[slot_of(-dy, fx, fc)],
            device_id=(g, wide_at(*off)), device_id_type=MESH,
        )

    def label_copy(off):
        dy, fx, fc = off
        return pltpu.make_async_remote_copy(
            src_ref=lab, dst_ref=labels_hbm.at[slot_of(-dy, fx, fc)],
            send_sem=lab_send.at[slot_of(*off)], recv_sem=lab_recv.at[slot_of(-dy, fx, fc)],
            device_id=(g, wide_at(*off)), device_id_type=MESH,
        )

    halos = []
    for side, (other, row_x, visc_at, vel_at, from_sp, from_u1, to) in enumerate(
        (
            (up, NX - 1, NX - 3, NX - 2, M + NX - 2, M + NX - 3, (1, 2, 2, 1)),
            (down, 0, 0, 0, M, M + 1, (M + NX, M + NX, M + NX, M + NX + 1)),
        )
    ):
        to_visc, to_vel, to_sp, to_u1 = to
        pairs = (
            (u1.at[:, pl.ds(from_u1, 2)], u1.at[:, pl.ds(to_u1, 2)]),
            (stress_hbm.at[pl.ds(0, 1), row_x], sx.at[side, pl.ds(0, 1)]),
            (stress_hbm.at[pl.ds(3, 2), row_x], sx.at[side, pl.ds(1, 2)]),
            (visc_hbm.at[pl.ds(visc_at, 3)], vi.at[pl.ds(to_visc, 3)]),
            (vel_hbm.at[:, pl.ds(vel_at, 2)], u0.at[:, pl.ds(to_vel, 2)]),
            (sp.at[:, pl.ds(from_sp, 2)], sp.at[:, pl.ds(to_sp, 2)]),
        )
        for i, (s, t) in enumerate(pairs):
            halos.append(
                pltpu.make_async_remote_copy(
                    src_ref=s, dst_ref=t,
                    send_sem=halo_send.at[side, i], recv_sem=halo_recv.at[side, i],
                    device_id=(other, wd), device_id_type=MESH,
                )
            )

    for copy in loads:
        copy.wait()
    force(M, 4)
    force(M + NX - 4, 4)
    lane = lax.broadcasted_iota(jnp.int32, (1, 128), 1)
    lab[...] = jnp.where(lane == 0, owner_ref[0, 0], owner_ref[0, 1])
    mask0 = mask_ref[0, 0].astype(F32)
    mask1 = mask_ref[0, 1].astype(F32)
    target0 = owner_ref[0, 0] // CP_DEV
    target1 = owner_ref[0, 1] // CP_DEV

    pl.semaphore_wait(barrier, len(others) + 2)
    for i, copy in enumerate(halos):
        if i % 6:
            copy.start()
    faces(5, 2)
    faces(M + NX - 3, 2)
    sweep(u0, u1, 5, 2)
    sweep(u0, u1, M + NX - 3, 2)
    halos[0].start()
    halos[6].start()

    faces(7, 40)
    force(8, 39)
    sweep(u0, u1, 7, 40)
    sweep(u1, u2, 6, 40)
    sweep(u2, u3, 7, 38)
    restrict(8, 36)
    send_main(0)
    own_label = pltpu.make_async_copy(lab, labels_hbm.at[0], out_sem.at[1])
    own_label.start()
    faces(47, 18)
    force(47, 17)
    sweep(u0, u1, 47, 18)
    sweep(u1, u2, 46, 20)
    sweep(u2, u3, 45, 20)
    restrict(44, 20)
    send_main(1)
    pass_on(0, "x", "own_up", "own_down")
    pass_on(1, "x", "own_up", "own_down")

    for copy in halos:
        copy.wait()
    inside_low = jnp.where(g > 0, 1.0, 0.0)
    inside_high = jnp.where(g < n_grp - 1, 1.0, 0.0)
    for at, swept, inside in ((1, 1, inside_low), (M + NX, M + NX + 1, inside_high)):
        here = pl.ds(swept, 2)
        u1[:, here] = u1[:, here] * inside
        here = pl.ds(2 if at == 1 else at, 2)
        u0[:, here] = u0[:, here] * inside
        here = pl.ds(at, 3)
        vi[here] = vi[here] * inside
    for c, comp in enumerate(DX_COMPS):
        sp[c, M] = sp[c, M] - (0.5 * inside_low) * sx[0, c]
        sp[c, M + NX - 1] = sp[c, M + NX - 1] + (0.5 * inside_high) * sx[1, c]
        sp[c, M - 1] = sp[c, M - 1] + 0.5 * st[comp, 1]
        sp[c, M + NX] = sp[c, M + NX] - 0.5 * st[comp, NX]
    faces(2, 2, inside_low)
    faces(M + NX, 2, inside_high)
    faces(M, 1)
    faces(M + NX - 1, 1)
    sweep(u0, u1, 3, 2)
    sweep(u0, u1, M + NX - 1, 2)
    for src, dst, shift in ((u1, u2, 2), (u2, u3, 3)):
        sweep(src, dst, shift, 4)
        sweep(src, dst, EX - 4 - shift, 4)
    store = pltpu.make_async_copy(u3.at[:, pl.ds(M, NX)], newvel_hbm, out_sem.at[0])
    store.start()
    restrict(M, 4)
    restrict(M + NX - 4, 4)
    p0, p1 = means(EDGE)
    for off in others + [(0, 0, 0)]:
        t = wide_at(*off)
        s0 = jnp.where(target0 == t, 1.0, 0.0)
        s1 = jnp.where(target1 == t, 1.0, 0.0)
        slots[slot_of(*off)] = p0 * s0 + p1 * s1
        if off != (0, 0, 0):
            edge_copy(off).start()
    own_edge = pltpu.make_async_copy(slots.at[0], edge_hbm.at[0], out_sem.at[2])
    own_edge.start()
    for off in others:
        label_copy(off).start()

    for k in range(len(MAIN)):
        pass_on(k, "x_down", "x_up")
    for k in range(len(MAIN)):
        pass_on(k, "far_own", "far_x")
    for k in range(len(MAIN)):
        for which in KINDS:
            main_copy(k, which).wait_send()
        for m8 in range(8):
            main_copy(k, f"s{m8}").wait_recv()
        own_copy(k).wait()
    for off in others:
        label_copy(off).wait()
        edge_copy(off).wait()
    own_label.wait()
    own_edge.wait()
    store.wait()


def sum_kernel(labels_ref, vel_hbm, main, edge, newvel_hbm, out_hbm, total, laid_out, sems):
    me = lax.axis_index("wide")
    move = pltpu.make_async_copy(vel_hbm, newvel_hbm, sems.at[3])
    move.start()
    total[...] = jnp.zeros_like(total)
    for d in range(N_WIDE):
        first, second = labels_ref[d, 0, 0], labels_ref[d, 0, 1]
        hit0 = first // CP_DEV == me
        hit1 = second // CP_DEV == me
        index = jnp.where(hit0, first, second) % CP_DEV
        patch = jnp.where(hit0, 0, 1)

        @pl.when(hit0 | hit1)
        def _():
            total[index, :120] = total[index, :120] + main[d, patch]
            total[index, 120:] = total[index, 120:] + edge[d]

    stores = []
    for c in range(3):
        for k in range(CP_DEV):
            start = c * 768 + (k // 8) * 384 + k % 8
            for first_row, chunks in ((0, MAIN), (120, (EDGE,))):
                for base, rows, pieces in chunks:
                    for at, tile, count in pieces:
                        laid_out[pl.ds(start + tile * 8, count, stride=8), :] = total[
                            k, pl.ds(first_row + base + c * rows + at, count), :
                        ]
        part = pl.ds(c * 768, 768)
        stores.append(pltpu.make_async_copy(laid_out.at[part], out_hbm.at[part], sems.at[c]))
        stores[-1].start()
    for store in stores:
        store.wait()
    move.wait()


def on_device(velocity, coarse_ghost, viscosity, stress, patch_mask, coarse_owner):
    n_grp = lax.axis_size("grp")
    hbm = pl.BlockSpec(memory_space=pltpu.HBM)
    vmem = pl.BlockSpec(memory_space=pltpu.VMEM)
    scalar_field = pltpu.VMEM((EX, 8, 128), F32)
    field = pltpu.VMEM((3, EX, 8, 128), F32)
    dma = pltpu.SemaphoreType.DMA
    operands = [
        pltpu.with_memory_space_constraint(a, pltpu.HBM)
        for a in (patch_mask, coarse_owner, velocity, coarse_ghost, viscosity, stress)
    ]
    new_velocity, main, edge, labels = pl.pallas_call(
        functools.partial(step_kernel, n_grp),
        out_shape=(
            jax.ShapeDtypeStruct((3, NX, 8, 128), F32),
            jax.ShapeDtypeStruct((N_WIDE, 2, 120, 128), F32),
            jax.ShapeDtypeStruct((N_WIDE, 24, 128), F32),
            jax.ShapeDtypeStruct((N_WIDE, 1, 128), jnp.int32),
        ),
        in_specs=[hbm] * 6,
        out_specs=(hbm,) * 4,
        scratch_shapes=[
            field, pltpu.VMEM((6, NX + 2, 8, 128), F32), pltpu.VMEM((2, 3, 8, 128), F32),
            scalar_field, pltpu.VMEM((3, NX, 2, 128), F32),
            *[scalar_field] * 9,
            field, field, field, field, field,
            pltpu.VMEM((3, 256, 128), F32), pltpu.VMEM((3, 256, 128), F32),
            pltpu.VMEM((96, 512), F32), pltpu.VMEM((512, 256), jnp.bfloat16),
            pltpu.VMEM((2, 120, 128), F32), pltpu.VMEM((N_WIDE, 24, 128), F32),
            pltpu.VMEM((1, 128), jnp.int32),
            pltpu.SMEM((1, 2), jnp.int32), pltpu.SMEM((1, 2), jnp.int32),
            dma((6,)),
            dma((2, 6)), dma((2, 6)),
            dma((N_WIDE,)), dma((N_WIDE,)), dma((N_WIDE,)), dma((N_WIDE,)),
            dma((2, 15)), dma((2, 15)),
            dma((6,)),
        ],
        compiler_params=pltpu.CompilerParams(
            collective_id=0, has_side_effects=True, vmem_limit_bytes=40 << 20
        ),
        name="smooth_and_send",
    )(*operands)
    new_velocity, coarse = pl.pallas_call(
        sum_kernel,
        out_shape=(
            jax.ShapeDtypeStruct((3, NX, 8, 128), F32),
            jax.ShapeDtypeStruct((2304, 128), F32),
        ),
        in_specs=[pl.BlockSpec(memory_space=pltpu.SMEM), hbm, vmem, vmem],
        out_specs=(hbm, hbm),
        scratch_shapes=[
            pltpu.VMEM((CP_DEV, 144, 128), F32), pltpu.VMEM((2304, 128), F32), dma((4,)),
        ],
        compiler_params=pltpu.CompilerParams(vmem_limit_bytes=40 << 20),
        name="sum_on_owners",
    )(labels, new_velocity, main, edge)
    coarse = coarse.reshape(3, 2, 48, 8, 128).transpose(1, 3, 0, 2, 4)
    return new_velocity, coarse.reshape(1, CP_DEV, 3, 48 * 128)


def solution(mesh):
    in_specs = (
        P(None, "grp", "wide", None),
        P(None, "grp", "wide", None),
        P("grp", "wide", None),
        P(None, "grp", "wide", None),
        P("grp", "wide"),
        P("grp", "wide"),
    )
    out_specs = (P(None, "grp", "wide", None), P("grp", "wide", None, None))
    return jax.shard_map(
        on_device, mesh=mesh, in_specs=in_specs, out_specs=out_specs, check_vma=False
    )
```

```python
import functools

import jax
import jax.numpy as jnp
from jax import lax
from jax.experimental import pallas as pl
from jax.experimental.pallas import tpu as pltpu
from jax.sharding import PartitionSpec as P

MESH = pl.DeviceIdType.MESH
F32 = jnp.float32

NX = 64
M = 4
EX = NX + 2 * M
KAPPA = 1.0
OMEGA = 0.8
CP_DEV = 16
N_WIDE = 16
DX_COMPS = (0, 3, 4)

MAIN = (
    (0, 24, ((0, 2, 8), (8, 10, 8), (16, 18, 2), (18, 33, 3), (21, 41, 3))),
    (72, 16, ((0, 20, 8), (8, 28, 2), (10, 36, 3), (13, 44, 3))),
)
EDGE = (0, 8, ((0, 0, 2), (2, 30, 2), (4, 32, 1), (5, 39, 1), (6, 40, 1), (7, 47, 1)))


def step_kernel(
    n_grp,
    mask_hbm, owner_hbm, vel_hbm, ghost_hbm, visc_hbm, stress_hbm,
    newvel_hbm, main_hbm, edge_hbm, labels_hbm,
    u0, st, sx, vi, gh, fe, fw, fn, fs, fu, fd, ww, dd, ve, sp, gv, u1, u2, u3, rs, fl,
    lhs, mat, own, slots, lab, mask_ref, owner_ref,
    in_sem, halo_send, halo_recv, lab_send, lab_recv, edge_send, edge_recv, main_send, main_recv,
    out_sem,
):
    g = lax.axis_index("grp")
    wd = lax.axis_index("wide")
    up = lax.rem(g + 1, n_grp)
    down = lax.rem(g + n_grp - 1, n_grp)
    y, x, core = wd // 4, (wd // 2) % 2, wd % 2

    def wide_at(dy, fx, fc):
        return (
            ((y + dy) % 4) * 4
            + (1 - x if fx else x) * 2
            + (1 - core if fc else core)
        )

    others = [(dy, fx, fc) for dy in (2, 1, 3, 0) for fx in (1, 0) for fc in (0, 1)]
    others.remove((0, 0, 0))

    def slot_of(dy, fx, fc):
        return ((dy % 4) * 2 + fx) * 2 + fc

    loads = [
        pltpu.make_async_copy(visc_hbm, vi.at[pl.ds(M, NX)], in_sem.at[2]),
        pltpu.make_async_copy(stress_hbm, st.at[:, pl.ds(1, NX)], in_sem.at[1]),
        pltpu.make_async_copy(vel_hbm, u0.at[:, pl.ds(M, NX)], in_sem.at[0]),
        pltpu.make_async_copy(ghost_hbm, gh, in_sem.at[3]),
        pltpu.make_async_copy(owner_hbm, owner_ref, in_sem.at[4]),
        pltpu.make_async_copy(mask_hbm, mask_ref, in_sem.at[5]),
    ]
    for copy in loads:
        copy.start()

    barrier = pltpu.get_barrier_semaphore()
    for other in (up, down):
        pl.semaphore_signal(barrier, inc=1, device_id=(other, wd), device_id_type=MESH)
    for off in others:
        pl.semaphore_signal(barrier, inc=1, device_id=(g, wide_at(*off)), device_id_type=MESH)

    row = lax.broadcasted_iota(jnp.int32, (512, 256), 0)
    col = lax.broadcasted_iota(jnp.int32, (512, 256), 1)
    same_q = lax.shift_right_logical(row, 7) == (lax.shift_right_logical(col, 5) & 3)
    z_pair = lax.shift_right_logical(row & 127, 1)
    z_want = lax.shift_right_logical(col, 7) * 32 + (col & 31)
    mat[...] = jnp.where(same_q & (z_pair == z_want), 1.0, 0.0).astype(jnp.bfloat16)
    for comp in DX_COMPS:
        st[comp, 0] = jnp.zeros((8, 128), F32)
        st[comp, NX + 1] = jnp.zeros((8, 128), F32)

    ypos = lax.broadcasted_iota(jnp.int32, (1, 8, 128), 1)
    not_last = ypos < 7
    not_first = ypos > 0

    def y_up(a):
        return pltpu.roll(a, 7, 1)

    def y_dn(a):
        return pltpu.roll(a, 1, 1)

    def z_up(a):
        return pltpu.roll(a, 127, 2)

    def z_dn(a):
        return pltpu.roll(a, 1, 2)

    def faces(lo, n, inside=None):
        here, after, before = pl.ds(lo, n), pl.ds(lo + 1, n), pl.ds(lo - 1, n)
        v = vi[here]
        f_e = 0.5 * (v + vi[after])
        f_w = 0.5 * (v + vi[before])
        f_n = jnp.where(not_last, 0.5 * (v + y_up(v)), 0.0)
        f_s = y_dn(f_n)
        f_u = 0.5 * (v + z_up(v))
        f_d = z_dn(f_u)
        v_edge = jnp.where(not_last & not_first, 0.0, v)
        diag = KAPPA + f_e + f_w + f_n + f_s + f_u + f_d + v_edge
        weight = OMEGA / diag
        if inside is not None:
            weight = weight * inside
        fe[here], fw[here], fn[here], fs[here], fu[here], fd[here] = f_e, f_w, f_n, f_s, f_u, f_d
        ww[here], dd[here] = weight, diag

    def force(lo, n):
        here, own_rows = pl.ds(lo, n), pl.ds(lo - M, n)
        mid, after, before = pl.ds(lo - 3, n), pl.ds(lo - 2, n), pl.ds(lo - 4, n)
        v_edge = jnp.where(not_last & not_first, 0.0, vi[here])
        ve[here] = v_edge

        def d_x(c):
            return st[c, after] - st[c, before]

        def d_y(a):
            return jnp.where(not_last, y_up(a), 0.0) - jnp.where(not_first, y_dn(a), 0.0)

        def d_z(a):
            return z_up(a) - z_dn(a)

        sxy, sxz, syz = st[3, mid], st[4, mid], st[5, mid]
        slopes = (
            d_x(0) + d_y(sxy) + d_z(sxz),
            d_x(3) + d_y(st[1, mid]) + d_z(syz),
            d_x(4) + d_y(syz) + d_z(st[2, mid]),
        )
        for c in range(3):
            low = jnp.broadcast_to(gh[c, own_rows, 0:1, :], (n, 8, 128))
            high = jnp.broadcast_to(gh[c, own_rows, 1:2, :], (n, 8, 128))
            edge = jnp.where(not_first, jnp.where(not_last, 0.0, high), low)
            gv[c, here] = edge
            sp[c, here] = KAPPA * u0[c, here] + 0.5 * slopes[c] + v_edge * edge

    def flow(src, lo, n):
        here, after, before = pl.ds(lo, n), pl.ds(lo + 1, n), pl.ds(lo - 1, n)
        f_e, f_w, f_n, f_s, f_u, f_d = fe[here], fw[here], fn[here], fs[here], fu[here], fd[here]
        for c in range(3):
            u = src[c, here]
            total = (
                (sp[c, here] + f_e * src[c, after] + f_w * src[c, before])
                + (f_n * y_up(u) + f_s * y_dn(u))
                + (f_u * z_up(u) + f_d * z_dn(u))
            )
            yield c, u, total

    def sweep(src, dst, lo, n):
        here = pl.ds(lo, n)
        weight = ww[here]
        for c, u, total in flow(src, lo, n):
            dst[c, here] = (1.0 - OMEGA) * u + weight * total

    def restrict(lo, n):
        here = pl.ds(lo, n)
        diag, v_edge = dd[here], ve[here]
        half = n // 2
        pairs = pl.ds((lo - M) * 4, half * 8)
        for c, u, total in flow(u3, lo, n):
            res = (total - diag * u).reshape(half, 2, 8, 128)
            res = res[:, 0] + res[:, 1]
            res = res + y_up(res)
            rs[c, pairs] = res.reshape(half * 8, 128)
            flux = (v_edge * (u - gv[c, here])).reshape(half, 2, 8, 128)
            fl[c, pairs] = (flux[:, 0] + flux[:, 1]).reshape(half * 8, 128)

    def means(chunk):
        base, rows, pieces = chunk
        for c in range(3):
            for at, tile, count in pieces:
                for q in range(4):
                    if tile < 32:
                        piece = rs[c, pl.ds(tile * 8 + 2 * q, count, stride=8), :] * 0.125
                    else:
                        fr, yy, sign = (tile - 32, 0, 0.25) if tile < 40 else (tile - 40, 7, -0.25)
                        piece = fl[c, pl.ds(fr * 32 + q * 8 + yy, count, stride=32), :] * sign
                    lhs[pl.ds(c * rows + at, count), pl.ds(q * 128, 128)] = piece
        full = lhs[pl.ds(0, 3 * rows), :]
        high = full.astype(jnp.bfloat16)
        low = (full - high.astype(F32)).astype(jnp.bfloat16)
        m = mat[...]
        out = jnp.dot(high, m, preferred_element_type=F32) + jnp.dot(
            low, m, preferred_element_type=F32
        )
        return out[:, :128] * mask0, out[:, 128:] * mask1

    def main_copy(k, which):
        base, rows, _ = MAIN[k]
        part = pl.ds(base, 3 * rows)

        def held(m8):
            return main_hbm.at[2 * m8, :, part]

        mine = own.at[:, part]
        source, at, target = {
            "x": (mine, 2 * 1, (0, 1, 0)),
            "own_up": (mine, 2 * 6, (1, 0, 0)),
            "own_down": (mine, 2 * 2, (3, 0, 0)),
            "x_up": (held(1), 2 * 7, (1, 0, 0)),
            "x_down": (held(1), 2 * 3, (3, 0, 0)),
            "far_own": (held(6), 2 * 4, (1, 0, 0)),
            "far_x": (held(3), 2 * 5, (3, 0, 0)),
            "s0": (mine, 1, (0, 0, 1)),
            **{f"s{m8}": (held(m8), 2 * m8 + 1, (0, 0, 1)) for m8 in range(1, 8)},
        }[which]
        index = KINDS.index(which)
        return pltpu.make_async_remote_copy(
            src_ref=source, dst_ref=main_hbm.at[at, :, part],
            send_sem=main_send.at[k, index], recv_sem=main_recv.at[k, index],
            device_id=(g, wide_at(*target)), device_id_type=MESH,
        )

    ARRIVALS = (
        ("x", ("x_up", "x_down", "s1")),
        ("own_up", ("far_own", "s6")),
        ("own_down", ("s2",)),
        ("x_down", ("far_x", "s3")),
        ("x_up", ("s7",)),
        ("far_own", ("s4",)),
        ("far_x", ("s5",)),
    )
    KINDS = [name for name, _ in ARRIVALS] + [f"s{m8}" for m8 in range(8)]

    def own_copy(k):
        base, rows, _ = MAIN[k]
        part = pl.ds(base, 3 * rows)
        return pltpu.make_async_copy(own.at[:, part], main_hbm.at[0, :, part], out_sem.at[3 + k])

    def send_main(k):
        base, rows, _ = MAIN[k]
        p0, p1 = means(MAIN[k])
        own[0, pl.ds(base, 3 * rows), :] = p0
        own[1, pl.ds(base, 3 * rows), :] = p1
        for which in ("x", "own_up", "own_down", "s0"):
            main_copy(k, which).start()
        own_copy(k).start()

    def pass_on(k, *arrivals):
        for name, then in ARRIVALS:
            if name in arrivals:
                main_copy(k, name).wait_recv()
                for which in then:
                    main_copy(k, which).start()

    def edge_copy(off):
        dy, fx, fc = off
        index = slot_of(*off)
        return pltpu.make_async_remote_copy(
            src_ref=slots.at[index], dst_ref=edge_hbm.at[slot_of(-dy, fx, fc)],
            send_sem=edge_send.at[index], recv_sem=edge_recv.at[slot_of(-dy, fx, fc)],
            device_id=(g, wide_at(*off)), device_id_type=MESH,
        )

    def label_copy(off):
        dy, fx, fc = off
        return pltpu.make_async_remote_copy(
            src_ref=lab, dst_ref=labels_hbm.at[slot_of(-dy, fx, fc)],
            send_sem=lab_send.at[slot_of(*off)], recv_sem=lab_recv.at[slot_of(-dy, fx, fc)],
            device_id=(g, wide_at(*off)), device_id_type=MESH,
        )

    halos = []
    for side, (other, row_x, visc_at, vel_at, from_sp, from_u1, to) in enumerate(
        (
            (up, NX - 1, NX - 3, NX - 2, M + NX - 2, M + NX - 3, (1, 2, 2, 1)),
            (down, 0, 0, 0, M, M + 1, (M + NX, M + NX, M + NX, M + NX + 1)),
        )
    ):
        to_visc, to_vel, to_sp, to_u1 = to
        pairs = (
            (u1.at[:, pl.ds(from_u1, 2)], u1.at[:, pl.ds(to_u1, 2)]),
            (stress_hbm.at[pl.ds(0, 1), row_x], sx.at[side, pl.ds(0, 1)]),
            (stress_hbm.at[pl.ds(3, 2), row_x], sx.at[side, pl.ds(1, 2)]),
            (visc_hbm.at[pl.ds(visc_at, 3)], vi.at[pl.ds(to_visc, 3)]),
            (vel_hbm.at[:, pl.ds(vel_at, 2)], u0.at[:, pl.ds(to_vel, 2)]),
            (sp.at[:, pl.ds(from_sp, 2)], sp.at[:, pl.ds(to_sp, 2)]),
        )
        for i, (s, t) in enumerate(pairs):
            halos.append(
                pltpu.make_async_remote_copy(
                    src_ref=s, dst_ref=t,
                    send_sem=halo_send.at[side, i], recv_sem=halo_recv.at[side, i],
                    device_id=(other, wd), device_id_type=MESH,
                )
            )

    for copy in loads:
        copy.wait()
    force(M, 4)
    force(M + NX - 4, 4)
    lane = lax.broadcasted_iota(jnp.int32, (1, 128), 1)
    lab[...] = jnp.where(lane == 0, owner_ref[0, 0], owner_ref[0, 1])
    mask0 = mask_ref[0, 0].astype(F32)
    mask1 = mask_ref[0, 1].astype(F32)
    target0 = owner_ref[0, 0] // CP_DEV
    target1 = owner_ref[0, 1] // CP_DEV

    pl.semaphore_wait(barrier, len(others) + 2)
    for i, copy in enumerate(halos):
        if i % 6:
            copy.start()
    faces(5, 2)
    faces(M + NX - 3, 2)
    sweep(u0, u1, 5, 2)
    sweep(u0, u1, M + NX - 3, 2)
    halos[0].start()
    halos[6].start()

    faces(7, 40)
    force(8, 39)
    sweep(u0, u1, 7, 40)
    sweep(u1, u2, 6, 40)
    sweep(u2, u3, 7, 38)
    restrict(8, 36)
    send_main(0)
    own_label = pltpu.make_async_copy(lab, labels_hbm.at[0], out_sem.at[1])
    own_label.start()
    faces(47, 18)
    force(47, 17)
    sweep(u0, u1, 47, 18)
    sweep(u1, u2, 46, 20)
    sweep(u2, u3, 45, 20)
    restrict(44, 20)
    send_main(1)
    pass_on(0, "x", "own_up", "own_down")
    pass_on(1, "x", "own_up", "own_down")

    for copy in halos:
        copy.wait()
    inside_low = jnp.where(g > 0, 1.0, 0.0)
    inside_high = jnp.where(g < n_grp - 1, 1.0, 0.0)
    for at, swept, inside in ((1, 1, inside_low), (M + NX, M + NX + 1, inside_high)):
        here = pl.ds(swept, 2)
        u1[:, here] = u1[:, here] * inside
        here = pl.ds(2 if at == 1 else at, 2)
        u0[:, here] = u0[:, here] * inside
        here = pl.ds(at, 3)
        vi[here] = vi[here] * inside
    for c, comp in enumerate(DX_COMPS):
        sp[c, M] = sp[c, M] - (0.5 * inside_low) * sx[0, c]
        sp[c, M + NX - 1] = sp[c, M + NX - 1] + (0.5 * inside_high) * sx[1, c]
        sp[c, M - 1] = sp[c, M - 1] + 0.5 * st[comp, 1]
        sp[c, M + NX] = sp[c, M + NX] - 0.5 * st[comp, NX]
    faces(2, 2, inside_low)
    faces(M + NX, 2, inside_high)
    faces(M, 1)
    faces(M + NX - 1, 1)
    sweep(u0, u1, 3, 2)
    sweep(u0, u1, M + NX - 1, 2)
    for src, dst, shift in ((u1, u2, 2), (u2, u3, 3)):
        sweep(src, dst, shift, 4)
        sweep(src, dst, EX - 4 - shift, 4)
    store = pltpu.make_async_copy(u3.at[:, pl.ds(M, NX)], newvel_hbm, out_sem.at[0])
    store.start()
    restrict(M, 4)
    restrict(M + NX - 4, 4)
    p0, p1 = means(EDGE)
    for off in others + [(0, 0, 0)]:
        t = wide_at(*off)
        s0 = jnp.where(target0 == t, 1.0, 0.0)
        s1 = jnp.where(target1 == t, 1.0, 0.0)
        slots[slot_of(*off)] = p0 * s0 + p1 * s1
        if off != (0, 0, 0):
            edge_copy(off).start()
    own_edge = pltpu.make_async_copy(slots.at[0], edge_hbm.at[0], out_sem.at[2])
    own_edge.start()
    for off in others:
        label_copy(off).start()

    for k in range(len(MAIN)):
        pass_on(k, "x_down", "x_up")
    for k in range(len(MAIN)):
        pass_on(k, "far_own", "far_x")
    for k in range(len(MAIN)):
        for which in KINDS:
            main_copy(k, which).wait_send()
        for m8 in range(8):
            main_copy(k, f"s{m8}").wait_recv()
        own_copy(k).wait()
    for off in others:
        label_copy(off).wait()
        edge_copy(off).wait()
    own_label.wait()
    own_edge.wait()
    store.wait()


def sum_kernel(labels_ref, vel_hbm, main, edge, newvel_hbm, out_hbm, total, laid_out, sems):
    me = lax.axis_index("wide")
    move = pltpu.make_async_copy(vel_hbm, newvel_hbm, sems.at[6])
    move.start()
    total[...] = jnp.zeros_like(total)
    for d in range(N_WIDE):
        first, second = labels_ref[d, 0, 0], labels_ref[d, 0, 1]
        hit0 = first // CP_DEV == me
        hit1 = second // CP_DEV == me
        index = jnp.where(hit0, first, second) % CP_DEV
        patch = jnp.where(hit0, 0, 1)

        @pl.when(hit0 | hit1)
        def _():
            total[index, :120] = total[index, :120] + main[d, patch]
            total[index, 120:] = total[index, 120:] + edge[d]

    stores = []
    for piece in range(6):
        c, half = piece // 2, piece % 2
        for k in range(8 * half, 8 * half + 8):
            start = piece * 384 + k % 8
            for first_row, chunks in ((0, MAIN), (120, (EDGE,))):
                for base, rows, pieces in chunks:
                    for at, tile, count in pieces:
                        laid_out[pl.ds(start + tile * 8, count, stride=8), :] = total[
                            k, pl.ds(first_row + base + c * rows + at, count), :
                        ]
        part = pl.ds(piece * 384, 384)
        stores.append(pltpu.make_async_copy(laid_out.at[part], out_hbm.at[part], sems.at[piece]))
        stores[-1].start()
    for store in stores:
        store.wait()
    move.wait()


def on_device(velocity, coarse_ghost, viscosity, stress, patch_mask, coarse_owner):
    n_grp = lax.axis_size("grp")
    hbm = pl.BlockSpec(memory_space=pltpu.HBM)
    vmem = pl.BlockSpec(memory_space=pltpu.VMEM)
    scalar_field = pltpu.VMEM((EX, 8, 128), F32)
    field = pltpu.VMEM((3, EX, 8, 128), F32)
    dma = pltpu.SemaphoreType.DMA
    operands = [
        pltpu.with_memory_space_constraint(a, pltpu.HBM)
        for a in (patch_mask, coarse_owner, velocity, coarse_ghost, viscosity, stress)
    ]
    new_velocity, main, edge, labels = pl.pallas_call(
        functools.partial(step_kernel, n_grp),
        out_shape=(
            jax.ShapeDtypeStruct((3, NX, 8, 128), F32),
            jax.ShapeDtypeStruct((N_WIDE, 2, 120, 128), F32),
            jax.ShapeDtypeStruct((N_WIDE, 24, 128), F32),
            jax.ShapeDtypeStruct((N_WIDE, 1, 128), jnp.int32),
        ),
        in_specs=[hbm] * 6,
        out_specs=(hbm,) * 4,
        scratch_shapes=[
            field, pltpu.VMEM((6, NX + 2, 8, 128), F32), pltpu.VMEM((2, 3, 8, 128), F32),
            scalar_field, pltpu.VMEM((3, NX, 2, 128), F32),
            *[scalar_field] * 9,
            field, field, field, field, field,
            pltpu.VMEM((3, 256, 128), F32), pltpu.VMEM((3, 256, 128), F32),
            pltpu.VMEM((96, 512), F32), pltpu.VMEM((512, 256), jnp.bfloat16),
            pltpu.VMEM((2, 120, 128), F32), pltpu.VMEM((N_WIDE, 24, 128), F32),
            pltpu.VMEM((1, 128), jnp.int32),
            pltpu.SMEM((1, 2), jnp.int32), pltpu.SMEM((1, 2), jnp.int32),
            dma((6,)),
            dma((2, 6)), dma((2, 6)),
            dma((N_WIDE,)), dma((N_WIDE,)), dma((N_WIDE,)), dma((N_WIDE,)),
            dma((2, 15)), dma((2, 15)),
            dma((6,)),
        ],
        compiler_params=pltpu.CompilerParams(
            collective_id=0, has_side_effects=True, vmem_limit_bytes=40 << 20
        ),
        name="smooth_and_send",
    )(*operands)
    new_velocity, coarse = pl.pallas_call(
        sum_kernel,
        out_shape=(
            jax.ShapeDtypeStruct((3, NX, 8, 128), F32),
            jax.ShapeDtypeStruct((2304, 128), F32),
        ),
        in_specs=[pl.BlockSpec(memory_space=pltpu.SMEM), hbm, vmem, vmem],
        out_specs=(hbm, hbm),
        scratch_shapes=[
            pltpu.VMEM((CP_DEV, 144, 128), F32), pltpu.VMEM((2304, 128), F32), dma((7,)),
        ],
        compiler_params=pltpu.CompilerParams(vmem_limit_bytes=40 << 20),
        name="sum_on_owners",
    )(labels, new_velocity, main, edge)
    coarse = coarse.reshape(3, 2, 48, 8, 128).transpose(1, 3, 0, 2, 4)
    return new_velocity, coarse.reshape(1, CP_DEV, 3, 48 * 128)


def solution(mesh):
    in_specs = (
        P(None, "grp", "wide", None),
        P(None, "grp", "wide", None),
        P("grp", "wide", None),
        P(None, "grp", "wide", None),
        P("grp", "wide"),
        P("grp", "wide"),
    )
    out_specs = (P(None, "grp", "wide", None), P("grp", "wide", None, None))
    return jax.shard_map(
        on_device, mesh=mesh, in_specs=in_specs, out_specs=out_specs, check_vma=False
    )
```
